256 devices in a mesh: expert: 64 (over y, z, core), dp: 4 (over x).
Axes of the slice: x: 4, y: 4, z: 8, core: 2. Of those that a mesh axis runs over, the one named last changes fastest.
Arguments:
- tokens_in: bfloat16 [65536, 1024], P(('expert', 'dp')), may hold values from -6 to 6
- out_grad: bfloat16 [65536, 1024], P(('expert', 'dp')), may hold values from -4 to 4
- gates: bfloat16 [65536], P(('expert', 'dp')), may hold values from 0.19921875 to 1
- expert_ids: int32 [65536], P(('expert', 'dp')), may hold values from 0 to 31, as said below
- slot_ids: int32 [65536], P(('expert', 'dp')), may hold values from 0 to 8
- w_up: bfloat16 [64, 1024, 1024], P('expert'), may hold values from -0.1875 to 0.1875
- w_down: bfloat16 [64, 1024, 1024], P('expert'), may hold values from -0.125 to 0.125
Outputs:
- in_grad: bfloat16 [65536, 1024], P(('expert', 'dp'))
- gate_grad: bfloat16 [65536], P(('expert', 'dp'))
- up_grad: bfloat16 [64, 1024, 1024], P('expert', 'dp')
- down_grad: bfloat16 [64, 1024, 1024], P('expert', 'dp')
The draws below stay inside these ranges and needn't reach their ends.
Inputs may be any that keep to these rules, and one draw needn't show every extreme that they name: `expert_ids`: the tokens of one device (aligned blocks of 256) take distinct pairs of expert and slot; no expert receives more than 9 tokens of one device, and one expert receives exactly 9 from every device.
All inputs are finite; a program needn't handle non-finite values.
Results may differ from the reference program's by a relative error of at most 0.015.
Values may be sent and summed in bfloat16 or wider, within the bound.
No kernel may reach another device: no remote copies, remote signals or barrier semaphores. Data moves between devices by JAX's collectives and lax.ppermute only.
A program may use at most 64 MiB of HBM per device.

```python
import jax
import jax.numpy as jnp
from jax import lax

D = 1024
H = 2048
TOK_DEV = 256
H_DEV = 1024
EXPERTS = 32
PIECES = 64
CAP = 9
REPLICAS = 4
TOKENS = 65536
EXP_ROWS = 2304
N_EXPERT = 64


def routing_pairs(key):
    base = jax.random.fold_in(key, 4177)
    key_load, key_full, key_noise, key_order = jax.random.split(base, 4)
    blocks = TOKENS // TOK_DEV
    cells = EXPERTS * CAP
    level = jax.random.randint(key_load, (EXPERTS,), 0, 4)
    full_one = jax.random.randint(key_full, (), 0, EXPERTS)
    level = jnp.where(jnp.arange(EXPERTS, dtype=jnp.int32) == full_one, 64, level)
    noise = jax.random.randint(key_noise, (blocks, cells), 0, 16384)
    cell_ids = jnp.arange(cells, dtype=jnp.int32)
    score = (jnp.repeat(level, CAP)[None, :] * 4096 + noise) * cells + cell_ids[None, :]
    chosen = lax.top_k(score, TOK_DEV)[1].astype(jnp.int32)
    order_keys = jax.random.split(key_order, blocks)
    orders = jax.vmap(lambda k: jax.random.permutation(k, TOK_DEV))(order_keys)
    chosen = jnp.take_along_axis(chosen, orders.astype(jnp.int32), axis=1)
    experts_of = (chosen // CAP).reshape(TOKENS).astype(jnp.int32)
    slots_of = (chosen % CAP).reshape(TOKENS).astype(jnp.int32)
    return (experts_of, slots_of)


def draw_expert_ids(key, part):
    return routing_pairs(key)[0]


def draw_slot_ids(key, part):
    return routing_pairs(key)[1]


def shard_levels(key, extent, pieces, least, top_value):
    level, own = 1.0, jax.random.fold_in(key, 6)
    for position, blocks in pieces:
        steps = jnp.exp(jax.random.uniform(jax.random.fold_in(own, position), (blocks,), jnp.float32, least / len(pieces), top_value / len(pieces)))
        level = level * jnp.repeat(steps, extent[position] // blocks).reshape([-1 if axis == position else 1 for axis in range(len(extent))])
    return level


def scatter_about(key, extent, width, bound, cuts=(), kind=jnp.bfloat16):
    loudness = shard_levels(key, extent, cuts, -0.22, 0.18) if cuts else 1.0
    drawn = jax.random.normal(key, extent, jnp.float32) * width * loudness
    return jnp.minimum(jnp.maximum(drawn, -bound), bound).astype(kind)


def setup_inputs(seed: int = 0) -> dict:
    seeds = jax.random.split(jax.random.key(seed), 8)
    tokens_in = scatter_about(seeds[0], (TOKENS, D), 1.0, 6.0, ((0, 256),))
    out_grad = scatter_about(seeds[1], (TOKENS, D), 0.5, 4.0, ((0, 256),))
    gates = jnp.clip(0.19921875 + 0.80078125 * jax.random.uniform(seeds[2], (TOKENS,), jnp.float32) ** shard_levels(seeds[2], (TOKENS,), ((0, 256),), -0.2, 0.2), 0.19921875, 1.0).astype(jnp.bfloat16)
    expert_ids = draw_expert_ids(jax.random.fold_in(seeds[7], 71), 0)
    slot_ids = draw_slot_ids(jax.random.fold_in(seeds[7], 71), 0)
    w_up = scatter_about(seeds[5], (PIECES, D, H_DEV), D ** -0.5, 0.1875, ((0, 64),))
    w_down = scatter_about(seeds[6], (PIECES, H_DEV, D), H ** -0.5, 0.125, ((0, 64),))
    return dict(tokens_in=tokens_in, out_grad=out_grad, gates=gates, expert_ids=expert_ids, slot_ids=slot_ids, w_up=w_up, w_down=w_down)


def gelu_parts(hidden):
    cdf = 0.5 * (1.0 + lax.erf(hidden * 0.7071067811865476))
    pdf = jnp.exp(-0.5 * hidden * hidden) * 0.3989422804014327
    return hidden * cdf, cdf + hidden * pdf


def group_sum(left, right):
    width_left = left.shape[1]
    width_right = right.shape[1]
    left_g = left.reshape(N_EXPERT, REPLICAS, CAP, width_left).transpose(1, 0, 2, 3).reshape(REPLICAS, N_EXPERT * CAP, width_left)
    right_g = right.reshape(N_EXPERT, REPLICAS, CAP, width_right).transpose(1, 0, 2, 3).reshape(REPLICAS, N_EXPERT * CAP, width_right)
    parts = []
    for group in range(REPLICAS):
        parts.append(jnp.dot(left_g[group].T, right_g[group], preferred_element_type=jnp.float32).astype(jnp.bfloat16))
    stacked = lax.optimization_barrier(jnp.stack(parts))
    return jnp.sum(stacked.astype(jnp.float32), axis=0).astype(jnp.bfloat16)


def reference(tokens_in, out_grad, gates, expert_ids, slot_ids, w_up, w_down):
    owner = (jnp.arange(TOKENS, dtype=jnp.int32) // TOK_DEV).astype(jnp.int32)
    place = (expert_ids * EXP_ROWS + owner * CAP + slot_ids).astype(jnp.int32)
    x_slots = jnp.zeros((EXPERTS * EXP_ROWS, D), jnp.bfloat16).at[place].set(tokens_in).reshape(EXPERTS, EXP_ROWS, D)
    g_slots = jnp.zeros((EXPERTS * EXP_ROWS, D), jnp.bfloat16).at[place].set(out_grad).reshape(EXPERTS, EXP_ROWS, D)
    gate_slots = jnp.zeros((EXPERTS * EXP_ROWS,), jnp.bfloat16).at[place].set(gates).reshape(EXPERTS, EXP_ROWS)
    up_pairs = w_up.reshape(EXPERTS, 2, D, H_DEV)
    down_pairs = w_down.reshape(EXPERTS, 2, H_DEV, D)

    def one_expert(items):
        x_rows, g_rows, gate_rows, up_pair, down_pair = items
        d_in = (gate_rows.astype(jnp.float32)[:, None] * g_rows.astype(jnp.float32)).astype(jnp.bfloat16)
        d_total = jnp.zeros((EXP_ROWS, D), jnp.float32)
        gate_total = jnp.zeros((EXP_ROWS,), jnp.float32)
        ups = []
        downs = []
        for half in range(2):
            hidden = jnp.dot(x_rows, up_pair[half], preferred_element_type=jnp.float32)
            value, slope = gelu_parts(hidden)
            act = value.astype(jnp.bfloat16)
            out_part = lax.optimization_barrier(jnp.dot(act, down_pair[half], preferred_element_type=jnp.float32).astype(jnp.bfloat16))
            gate_part = lax.optimization_barrier(jnp.sum(g_rows.astype(jnp.float32) * out_part.astype(jnp.float32), axis=-1).astype(jnp.bfloat16))
            d_act = jnp.dot(d_in, down_pair[half].T, preferred_element_type=jnp.float32)
            d_hidden = (d_act * slope).astype(jnp.bfloat16)
            d_part = lax.optimization_barrier(jnp.dot(d_hidden, up_pair[half].T, preferred_element_type=jnp.float32).astype(jnp.bfloat16))
            d_total = d_total + d_part.astype(jnp.float32)
            gate_total = gate_total + gate_part.astype(jnp.float32)
            ups.append(group_sum(x_rows, d_hidden))
            downs.append(group_sum(act, d_in))
        return d_total.astype(jnp.bfloat16), gate_total.astype(jnp.bfloat16), jnp.stack(ups), jnp.stack(downs)

    d_rows, gate_rows, up_grad, down_grad = lax.map(one_expert, (x_slots, g_slots, gate_slots, up_pairs, down_pairs))
    in_grad = d_rows.reshape(EXPERTS * EXP_ROWS, D)[place]
    gate_grad = gate_rows.reshape(EXPERTS * EXP_ROWS)[place]
    return in_grad, gate_grad, up_grad.reshape(PIECES, D, H_DEV), down_grad.reshape(PIECES, H_DEV, D)
```

```python
import functools

import jax
import jax.numpy as jnp
from jax import lax
from jax.experimental import pallas as pl
from jax.experimental.pallas import tpu as pltpu
from jax.sharding import Mesh, PartitionSpec as P

BF = jnp.bfloat16
F32 = jnp.float32
VMEM = 56 * 1024 * 1024
LANES = 128


def matmul(a, b, contract):
    return lax.dot_general(a, b, (contract, ((), ())), preferred_element_type=F32)


def slot_row(expert, slot, groups):
    return jnp.where(slot < 8, expert * 8 + slot, 8 * groups + expert)


def to_tiles(get, out_ref, base, groups, turn):
    for j in range(8):
        part = get(0, 8 * groups, j)
        out_ref[:, base + j] = part.reshape(groups, 8, LANES).astype(BF)
        turn[:, j, :] = get(8 * groups, 9 * groups, j)
    out_ref[:, base + 8] = turn[...].astype(BF)


def from_tiles(ref, base, dst_ref, row, groups, turn):
    turn[...] = ref[:, base + 8].astype(F32)
    for j in range(8):
        cols = slice(LANES * j, LANES * (j + 1))
        part = ref[:, base + j].astype(F32).reshape(8 * groups, LANES)
        dst_ref[row : row + 8 * groups, cols] = part.astype(BF)
        dst_ref[row + 8 * groups : row + 9 * groups, cols] = turn[:, j, :].astype(BF)


def pack_kernel(x_ref, g_ref, gate_ref, expert_ref, slot_ref, out_ref, full, turn):
    groups = out_ref.shape[0]
    count = x_ref.shape[0]
    place = slot_row(expert_ref[...], slot_ref[...], groups)
    rows = lax.broadcasted_iota(jnp.int32, (9 * groups, count), 0)
    hit = rows == place
    gate = gate_ref[...].astype(F32)
    for side, (ref, scale) in enumerate(((x_ref, 1.0), (g_ref, gate))):
        pick = jnp.where(hit, scale, 0.0).astype(BF)
        full[...] = matmul(pick, ref[...], ((1,), (0,)))
        to_tiles(
            lambda a, b, j: full[a:b, LANES * j : LANES * (j + 1)],
            out_ref,
            9 * side,
            groups,
            turn,
        )


def weight_parts(lhs_ref, rhs, me, fwd1, bwd1, fwd2, bwd2, own):
    half = own.shape[0] // 2
    size = 2 * half

    def chunk(step):
        at = pl.multiple_of(lax.rem(me + step, 4) * size, size)
        return matmul(lhs_ref[:, pl.ds(at, size)], rhs, ((0,), (0,))).astype(BF)

    far = chunk(2)
    fwd1[:half] = far[:half]
    bwd1[half:] = far[half:]
    right = chunk(1)
    fwd1[half:] = right[half:]
    fwd2[...] = right[:half]
    left = chunk(3)
    bwd1[:half] = left[:half]
    bwd2[...] = left[half:]
    own[...] = chunk(0)


def expert_kernel(
    mine_ref, other_ref, up_ref, down_ref, xs, dh, gate, fwd1, bwd1, fwd2, bwd2, own, ds, act, hid, dact, turn
):
    groups = mine_ref.shape[0]
    rows = 9 * groups
    for part, ref in enumerate((mine_ref, other_ref)):
        from_tiles(ref, 0, xs, part * rows, groups, turn)
        from_tiles(ref, 9, ds, part * rows, groups, turn)
    hid[...] = matmul(xs[...], up_ref[0], ((1,), (0,)))
    dact[...] = matmul(ds[...], down_ref[0], ((1,), (1,)))
    step = 32

    def block(i, carry):
        at = pl.ds(pl.multiple_of(i * step, step), step)
        v = hid[at, :]
        d = dact[at, :]
        cdf = 0.5 * (1.0 + lax.erf(v * 0.7071067811865476))
        pdf = jnp.exp(-0.5 * v * v) * 0.3989422804014327
        a = (v * cdf).astype(BF)
        act[at, :] = a
        dh[at, :] = (d * (cdf + v * pdf)).astype(BF)
        total = jnp.sum(a.astype(F32) * d, axis=1, keepdims=True)
        gate[at, :] = jnp.broadcast_to(total, (step, LANES))
        return carry

    lax.fori_loop(0, 2 * rows // step, block, 0)
    weight_parts(act, ds[...], lax.axis_index("dp"), fwd1, bwd1, fwd2, bwd2, own)


def up_kernel(xs, dh, fwd1, bwd1, fwd2, bwd2, own):
    weight_parts(xs, dh[...], lax.axis_index("dp"), fwd1, bwd1, fwd2, bwd2, own)


def input_kernel(dh, gate, up_ref, mine_ref, other_ref, full, turn):
    groups = mine_ref.shape[0]
    rows = 9 * groups
    full[...] = matmul(dh[...], up_ref[0], ((1,), (1,)))
    lane = lax.broadcasted_iota(jnp.int32, (groups, 8, LANES), 2)
    for part, ref in enumerate((mine_ref, other_ref)):
        at = part * rows
        to_tiles(
            lambda a, b, j: full[at + a : at + b, LANES * j : LANES * (j + 1)], ref, 0, groups, turn
        )
        last = gate[at + 8 * groups : at + rows, :]
        for j in range(8):
            turn[:, j, :] = last
        first = gate[at : at + 8 * groups, :].reshape(groups, 8, LANES)
        ref[:, 9] = jnp.where(lane < 64, first, turn[...]).astype(BF)


def unpack_kernel(back_ref, gate_ref, expert_ref, slot_ref, out_ref, gate_out_ref, rowbuf, turn):
    groups = back_ref.shape[0]
    count = out_ref.shape[0]
    from_tiles(back_ref, 0, rowbuf, 0, groups, turn)
    expert, slot = expert_ref[...], slot_ref[...]
    rows = lax.broadcasted_iota(jnp.int32, (9 * groups, count), 0)
    pick = jnp.where(rows == slot_row(expert, slot, groups), 1.0, 0.0).astype(BF)
    out_ref[...] = matmul(pick, rowbuf[...], ((0,), (0,))).astype(BF)
    gates = back_ref[:, 9].astype(F32).reshape(8 * groups, LANES).astype(BF)
    rows = lax.broadcasted_iota(jnp.int32, (8 * groups, count), 0)
    low = jnp.where(rows == slot_row(expert, slot, groups), 1.0, 0.0).astype(BF)
    high = jnp.where((rows == expert * 8) & (slot == 8), 1.0, 0.0).astype(BF)
    low = matmul(gates, low, ((0,), (0,)))
    high = matmul(gates, high, ((0,), (0,)))
    total = low[0:1, :] + high[64:65, :]
    gate_out_ref[...] = (total / gate_ref[...].astype(F32)).astype(BF)


def call(kernel, out, scratch, *args):
    whole = pl.BlockSpec(memory_space=pltpu.VMEM)
    return pl.pallas_call(
        kernel,
        out_shape=out,
        in_specs=[whole] * len(args),
        out_specs=jax.tree.map(lambda _: whole, out),
        scratch_shapes=scratch,
        compiler_params=pltpu.CompilerParams(vmem_limit_bytes=VMEM),
    )(*args)


def shape(*dims, dtype=BF):
    return jax.ShapeDtypeStruct(dims, dtype)


def scattered(parts):
    fwd1, bwd1, fwd2, bwd2, own = parts
    half = fwd2.shape[0]
    ahead = [(i, (i + 1) % 4) for i in range(4)]
    behind = [(i, (i + 3) % 4) for i in range(4)]
    left = lax.ppermute(fwd1, "dp", ahead)
    right = lax.ppermute(bwd1, "dp", behind)
    fwd2 = (fwd2.astype(F32) + left[:half].astype(F32)).astype(BF)
    bwd2 = (bwd2.astype(F32) + right[half:].astype(F32)).astype(BF)
    left2 = lax.ppermute(fwd2, "dp", ahead)
    right2 = lax.ppermute(bwd2, "dp", behind)
    wide = own.astype(F32)
    low = wide[:half] + right[:half].astype(F32) + left2.astype(F32)
    high = wide[half:] + left[half:].astype(F32) + right2.astype(F32)
    return jnp.concatenate([low, high], axis=0).astype(BF)


def on_device(tokens_in, out_grad, gates, expert_ids, slot_ids, w_up, w_down):
    groups = lax.axis_size("chip")
    count, width = tokens_in.shape
    hidden = w_up.shape[2]
    rows = 9 * groups
    expert_ids = expert_ids.reshape(1, count)
    slot_ids = slot_ids.reshape(1, count)
    gates = gates.reshape(1, count)
    turn = pltpu.VMEM((groups, 8, LANES), F32)
    swap = [(0, 1), (1, 0)]
    sent = call(
        pack_kernel,
        shape(groups, 18, 8, LANES),
        [pltpu.VMEM((rows, width), F32), turn],
        tokens_in,
        out_grad,
        gates,
        expert_ids,
        slot_ids,
    )
    mine = lax.all_to_all(sent, "chip", split_axis=0, concat_axis=0, tiled=True)
    other = lax.ppermute(mine, "core", swap)

    def parts(length, columns):
        quarter = length // 4
        return (
            shape(quarter, columns),
            shape(quarter, columns),
            shape(quarter // 2, columns),
            shape(quarter // 2, columns),
            shape(quarter, columns),
        )

    xs, dh, gate, *down = call(
        expert_kernel,
        (shape(2 * rows, width), shape(2 * rows, hidden), shape(2 * rows, LANES, dtype=F32))
        + parts(hidden, width),
        [
            pltpu.VMEM((2 * rows, width), BF),
            pltpu.VMEM((2 * rows, hidden), BF),
            pltpu.VMEM((2 * rows, hidden), F32),
            pltpu.VMEM((2 * rows, hidden), F32),
            turn,
        ],
        mine,
        other,
        w_up,
        w_down,
    )
    up = call(up_kernel, parts(width, hidden), [], xs, dh)
    keep, give = call(
        input_kernel,
        (shape(groups, 10, 8, LANES), shape(groups, 10, 8, LANES)),
        [pltpu.VMEM((2 * rows, width), F32), turn],
        dh,
        gate,
        w_up,
    )
    got = lax.ppermute(give, "core", swap)
    both = (keep.astype(F32) + got.astype(F32)).astype(BF)
    back = lax.all_to_all(both, "chip", split_axis=0, concat_axis=0, tiled=True)
    down_grad = scattered(down)
    up_grad = scattered(up)
    in_grad, gate_grad = call(
        unpack_kernel,
        (shape(count, width), shape(1, count)),
        [pltpu.VMEM((rows, width), BF), turn],
        back,
        gates,
        expert_ids,
        slot_ids,
    )
    return (in_grad, gate_grad.reshape(count), up_grad[None], down_grad[None])


def solution(mesh):
    chips = mesh.devices.reshape(mesh.shape["expert"] // 2, 2, mesh.shape["dp"])
    finer = Mesh(chips, ("chip", "core", "dp"))
    tokens = ("chip", "core", "dp")
    pieces = ("chip", "core")
    return jax.shard_map(
        on_device,
        mesh=finer,
        in_specs=(
            P(tokens, None),
            P(tokens, None),
            P(tokens),
            P(tokens),
            P(tokens),
            P(pieces, None, None),
            P(pieces, None, None),
        ),
        out_specs=(
            P(tokens, None),
            P(tokens),
            P(pieces, "dp", None),
            P(pieces, "dp", None),
        ),
        check_vma=False,
    )
```

```python
import functools

import jax
import jax.numpy as jnp
from jax import lax
from jax.experimental import pallas as pl
from jax.experimental.pallas import tpu as pltpu
from jax.sharding import Mesh, PartitionSpec as P

BF = jnp.bfloat16
F32 = jnp.float32
VMEM = 56 * 1024 * 1024
LANES = 128


def matmul(a, b, contract):
    return lax.dot_general(a, b, (contract, ((), ())), preferred_element_type=F32)


def slot_row(expert, slot, groups):
    return jnp.where(slot < 8, expert * 8 + slot, 8 * groups + expert)


def to_tiles(full, row, out_ref, groups, turn):
    last = row + 8 * groups
    for j in range(8):
        cols = slice(LANES * j, LANES * (j + 1))
        out_ref[:, j] = full[row:last, cols].reshape(groups, 8, LANES).astype(BF)
        turn[:, j, :] = full[last : last + groups, cols]
    out_ref[:, 8] = turn[...].astype(BF)


def from_tiles(ref, dst_ref, row, groups, turn):
    last = row + 8 * groups
    turn[...] = ref[:, 8].astype(F32)
    for j in range(8):
        cols = slice(LANES * j, LANES * (j + 1))
        dst_ref[row:last, cols] = ref[:, j].astype(F32).reshape(8 * groups, LANES).astype(BF)
        dst_ref[last : last + groups, cols] = turn[:, j, :].astype(BF)


def pack_x_kernel(x_ref, expert_ref, slot_ref, out_ref, full, turn):
    groups = out_ref.shape[0]
    place = slot_row(expert_ref[...], slot_ref[...], groups)
    hit = lax.broadcasted_iota(jnp.int32, (9 * groups, x_ref.shape[0]), 0) == place
    full[...] = matmul(jnp.where(hit, 1.0, 0.0).astype(BF), x_ref[...], ((1,), (0,)))
    to_tiles(full, 0, out_ref, groups, turn)


def pack_d_kernel(g_ref, gate_ref, expert_ref, slot_ref, out_ref, full, turn):
    groups = out_ref.shape[0]
    place = slot_row(expert_ref[...], slot_ref[...], groups)
    hit = lax.broadcasted_iota(jnp.int32, (9 * groups, g_ref.shape[0]), 0) == place
    scale = jnp.where(hit, gate_ref[...].astype(F32), 0.0).astype(BF)
    full[...] = matmul(scale, g_ref[...], ((1,), (0,)))
    to_tiles(full, 0, out_ref, groups, turn)


def weight_parts(lhs_ref, rhs, me, fwd1, bwd1, fwd2, bwd2, own):
    half = own.shape[0] // 2
    size = 2 * half

    def chunk(step):
        at = pl.multiple_of(lax.rem(me + step, 4) * size, size)
        return matmul(lhs_ref[:, pl.ds(at, size)], rhs, ((0,), (0,))).astype(BF)

    far = chunk(2)
    fwd1[:half] = far[:half]
    bwd1[half:] = far[half:]
    right = chunk(1)
    fwd1[half:] = right[half:]
    fwd2[...] = right[:half]
    left = chunk(3)
    bwd1[:half] = left[:half]
    bwd2[...] = left[half:]
    own[...] = chunk(0)


def hidden_kernel(mine_ref, other_ref, up_ref, xs, act, slope, hid, turn):
    groups = mine_ref.shape[0]
    rows = 9 * groups
    from_tiles(mine_ref, xs, 0, groups, turn)
    from_tiles(other_ref, xs, rows, groups, turn)
    hid[...] = matmul(xs[...], up_ref[0], ((1,), (0,)))
    step = 32

    def block(i, carry):
        at = pl.ds(pl.multiple_of(i * step, step), step)
        v = hid[at, :]
        cdf = 0.5 * (1.0 + lax.erf(v * 0.7071067811865476))
        pdf = jnp.exp(-0.5 * v * v) * 0.3989422804014327
        act[at, :] = (v * cdf).astype(BF)
        slope[at, :] = cdf + v * pdf
        return carry

    lax.fori_loop(0, 2 * rows // step, block, 0)


def backward(ds, down_ref, act, slope, row, dh, gate, dact):
    dact[...] = matmul(ds, down_ref[0], ((1,), (1,)))
    step = 32

    def block(i, carry):
        at = pl.ds(pl.multiple_of(i * step, step), step)
        there = pl.ds(pl.multiple_of(row + i * step, step), step)
        d = dact[at, :]
        dh[at, :] = (d * slope[there, :]).astype(BF)
        total = jnp.sum(act[there, :].astype(F32) * d, axis=1, keepdims=True)
        gate[at, :] = jnp.broadcast_to(total, (step, LANES))
        return carry

    lax.fori_loop(0, dact.shape[0] // step, block, 0)


def own_kernel(raw_ref, down_ref, act, slope, ds, dh, gate, dact, turn):
    from_tiles(raw_ref, ds, 0, raw_ref.shape[0], turn)
    backward(ds[...], down_ref, act, slope, 0, dh, gate, dact)


def down_kernel(own_ref, raw_ref, act, fwd1, bwd1, fwd2, bwd2, own, ds_other, ds, turn):
    rows = own_ref.shape[0]
    from_tiles(raw_ref, ds, rows, raw_ref.shape[0], turn)
    ds[:rows] = own_ref[...]
    ds_other[...] = ds[rows:]
    weight_parts(act, ds[...], lax.axis_index("dp"), fwd1, bwd1, fwd2, bwd2, own)


def to_part(dh, gate, up_ref, out_ref, full, turn):
    groups = out_ref.shape[0]
    full[...] = matmul(dh, up_ref[0], ((1,), (1,)))
    to_tiles(full, 0, out_ref, groups, turn)
    last = gate[8 * groups :, :]
    for j in range(8):
        turn[:, j, :] = last
    lane = lax.broadcasted_iota(jnp.int32, (groups, 8, LANES), 2)
    first = gate[: 8 * groups, :].reshape(groups, 8, LANES)
    out_ref[:, 9] = jnp.where(lane < 64, first, turn[...]).astype(BF)


def other_kernel(ds_ref, down_ref, act, slope, up_ref, dh, out_ref, gate, dact, turn):
    backward(ds_ref[...], down_ref, act, slope, ds_ref.shape[0], dh, gate, dact)
    to_part(dh[...], gate, up_ref, out_ref, dact, turn)


def part_kernel(dh, gate, up_ref, out_ref, full, turn):
    to_part(dh[...], gate, up_ref, out_ref, full, turn)


def up_kernel(xs, dh_own, dh_other, fwd1, bwd1, fwd2, bwd2, own, dh):
    rows = dh_own.shape[0]
    dh[:rows] = dh_own[...]
    dh[rows:] = dh_other[...]
    weight_parts(xs, dh[...], lax.axis_index("dp"), fwd1, bwd1, fwd2, bwd2, own)


def unpack_kernel(back_ref, gate_ref, expert_ref, slot_ref, out_ref, gate_out_ref, rowbuf, turn):
    groups = back_ref.shape[0]
    count = out_ref.shape[0]
    from_tiles(back_ref, rowbuf, 0, groups, turn)
    expert, slot = expert_ref[...], slot_ref[...]
    rows = lax.broadcasted_iota(jnp.int32, (9 * groups, count), 0)
    pick = jnp.where(rows == slot_row(expert, slot, groups), 1.0, 0.0).astype(BF)
    out_ref[...] = matmul(pick, rowbuf[...], ((0,), (0,))).astype(BF)
    gates = back_ref[:, 9].astype(F32).reshape(8 * groups, LANES).astype(BF)
    rows = lax.broadcasted_iota(jnp.int32, (8 * groups, count), 0)
    low = jnp.where(rows == slot_row(expert, slot, groups), 1.0, 0.0).astype(BF)
    high = jnp.where((rows == expert * 8) & (slot == 8), 1.0, 0.0).astype(BF)
    low = matmul(gates, low, ((0,), (0,)))
    high = matmul(gates, high, ((0,), (0,)))
    total = low[0:1, :] + high[64:65, :]
    gate_out_ref[...] = (total / gate_ref[...].astype(F32)).astype(BF)


def call(kernel, out, scratch, *args):
    whole = pl.BlockSpec(memory_space=pltpu.VMEM)
    return pl.pallas_call(
        kernel,
        out_shape=out,
        in_specs=[whole] * len(args),
        out_specs=jax.tree.map(lambda _: whole, out),
        scratch_shapes=scratch,
        compiler_params=pltpu.CompilerParams(vmem_limit_bytes=VMEM),
    )(*args)


def after(value, earlier):
    return lax.optimization_barrier((value, earlier))[0]


def shape(*dims, dtype=BF):
    return jax.ShapeDtypeStruct(dims, dtype)


def scattered(parts):
    fwd1, bwd1, fwd2, bwd2, own = parts
    half = fwd2.shape[0]
    ahead = [(i, (i + 1) % 4) for i in range(4)]
    behind = [(i, (i + 3) % 4) for i in range(4)]
    left = lax.ppermute(fwd1, "dp", ahead)
    right = lax.ppermute(bwd1, "dp", behind)
    fwd2 = (fwd2.astype(F32) + left[:half].astype(F32)).astype(BF)
    bwd2 = (bwd2.astype(F32) + right[half:].astype(F32)).astype(BF)
    left2 = lax.ppermute(fwd2, "dp", ahead)
    right2 = lax.ppermute(bwd2, "dp", behind)
    wide = own.astype(F32)
    low = wide[:half] + right[:half].astype(F32) + left2.astype(F32)
    high = wide[half:] + left[half:].astype(F32) + right2.astype(F32)
    return jnp.concatenate([low, high], axis=0).astype(BF)


def on_device(tokens_in, out_grad, gates, expert_ids, slot_ids, w_up, w_down):
    groups = lax.axis_size("chip")
    count, width = tokens_in.shape
    hidden = w_up.shape[2]
    rows = 9 * groups
    expert_ids = expert_ids.reshape(1, count)
    slot_ids = slot_ids.reshape(1, count)
    gates = gates.reshape(1, count)
    turn = pltpu.VMEM((groups, 8, LANES), F32)
    swap = [(0, 1), (1, 0)]
    blocks = shape(groups, 9, 8, LANES)
    full = pltpu.VMEM((rows, width), F32)

    def exchange(values):
        return lax.all_to_all(values, "chip", split_axis=0, concat_axis=0, tiled=True)

    def parts(length, columns):
        quarter = length // 4
        return (
            shape(quarter, columns),
            shape(quarter, columns),
            shape(quarter // 2, columns),
            shape(quarter // 2, columns),
            shape(quarter, columns),
        )

    x_mine = exchange(call(pack_x_kernel, blocks, [full, turn], tokens_in, expert_ids, slot_ids))
    d_sent = call(pack_d_kernel, blocks, [full, turn], out_grad, gates, expert_ids, slot_ids)
    x_other = lax.ppermute(x_mine, "core", swap)
    d_mine = exchange(d_sent)
    xs, act, slope = call(
        hidden_kernel,
        (shape(2 * rows, width), shape(2 * rows, hidden), shape(2 * rows, hidden, dtype=F32)),
        [pltpu.VMEM((2 * rows, hidden), F32), turn],
        x_mine,
        x_other,
        w_up,
    )
    d_mine = after(d_mine, act)
    d_other = lax.ppermute(d_mine, "core", swap)
    half = (shape(rows, hidden), shape(rows, LANES, dtype=F32))
    back = pltpu.VMEM((rows, hidden), F32)
    ds_own, dh_own, gate_own = call(
        own_kernel, (shape(rows, width),) + half, [back, turn], d_mine, w_down, act, slope
    )
    *down, ds_other = call(
        down_kernel,
        parts(hidden, width) + (shape(rows, width),),
        [pltpu.VMEM((2 * rows, width), BF), turn],
        ds_own,
        d_other,
        act,
    )
    returned = shape(groups, 10, 8, LANES)
    dh_other, give = call(
        other_kernel,
        (shape(rows, hidden), returned),
        [pltpu.VMEM((rows, LANES), F32), back, turn],
        ds_other,
        w_down,
        act,
        slope,
        w_up,
    )
    got = lax.ppermute(give, "core", swap)
    keep = call(part_kernel, returned, [full, turn], dh_own, gate_own, w_up)
    both = (keep.astype(F32) + got.astype(F32)).astype(BF)
    back = exchange(both)
    xs = after(xs, both)
    up = call(
        up_kernel, parts(width, hidden), [pltpu.VMEM((2 * rows, hidden), BF)], xs, dh_own, dh_other
    )
    down_grad = scattered(down)
    up_grad = scattered(up)
    in_grad, gate_grad = call(
        unpack_kernel,
        (shape(count, width), shape(1, count)),
        [pltpu.VMEM((rows, width), BF), turn],
        back,
        gates,
        expert_ids,
        slot_ids,
    )
    return (in_grad, gate_grad.reshape(count), up_grad[None], down_grad[None])


def solution(mesh):
    chips = mesh.devices.reshape(mesh.shape["expert"] // 2, 2, mesh.shape["dp"])
    finer = Mesh(chips, ("chip", "core", "dp"))
    tokens = ("chip", "core", "dp")
    pieces = ("chip", "core")
    return jax.shard_map(
        on_device,
        mesh=finer,
        in_specs=(
            P(tokens, None),
            P(tokens, None),
            P(tokens),
            P(tokens),
            P(tokens),
            P(pieces, None, None),
            P(pieces, None, None),
        ),
        out_specs=(
            P(tokens, None),
            P(tokens),
            P(pieces, "dp", None),
            P(pieces, "dp", None),
        ),
        check_vma=False,
    )
```

```python
import functools

import jax
import jax.numpy as jnp
from jax import lax
from jax.experimental import pallas as pl
from jax.experimental.pallas import tpu as pltpu
from jax.sharding import Mesh, PartitionSpec as P

BF = jnp.bfloat16
F32 = jnp.float32
VMEM = 56 * 1024 * 1024
LANES = 128


def matmul(a, b, contract):
    return lax.dot_general(a, b, (contract, ((), ())), preferred_element_type=F32)


def slot_row(expert, slot, groups):
    return jnp.where(slot < 8, expert * 8 + slot, 8 * groups + expert)


def to_tiles(full, row, out_ref, base, groups, turn):
    last = row + 8 * groups
    for j in range(8):
        cols = slice(LANES * j, LANES * (j + 1))
        out_ref[:, base + j] = full[row:last, cols].reshape(groups, 8, LANES).astype(BF)
        turn[:, j, :] = full[last : last + groups, cols]
    out_ref[:, base + 8] = turn[...].astype(BF)


def from_tiles(ref, base, dst_ref, groups, turn):
    last = 8 * groups
    turn[...] = ref[:, base + 8].astype(F32)
    for j in range(8):
        cols = slice(LANES * j, LANES * (j + 1))
        dst_ref[:last, cols] = ref[:, base + j].astype(F32).reshape(last, LANES).astype(BF)
        dst_ref[last : last + groups, cols] = turn[:, j, :].astype(BF)


def pack_kernel(x_ref, g_ref, gate_ref, expert_ref, slot_ref, out_ref, full, turn):
    groups = out_ref.shape[0]
    count = x_ref.shape[0]
    place = slot_row(expert_ref[...], slot_ref[...], groups).reshape(1, count)
    hit = lax.broadcasted_iota(jnp.int32, (9 * groups, count), 0) == place
    full[...] = matmul(jnp.where(hit, 1.0, 0.0).astype(BF), x_ref[...], ((1,), (0,)))
    to_tiles(full, 0, out_ref, 0, groups, turn)
    gate = gate_ref[...].astype(F32).reshape(1, count)
    full[...] = matmul(jnp.where(hit, gate, 0.0).astype(BF), g_ref[...], ((1,), (0,)))
    to_tiles(full, 0, out_ref, 9, groups, turn)


def turn_kernel(up_ref, down_ref, up_out, down_out):
    up_out[...] = up_ref[0].T
    down_out[...] = down_ref[0].T


def weight_parts(lhs_ref, rhs, me, fwd1, bwd1, fwd2, bwd2, own):
    half = own.shape[0] // 2
    size = 2 * half

    def chunk(step):
        at = pl.multiple_of(lax.rem(me + step, 4) * size, size)
        return matmul(lhs_ref[:, pl.ds(at, size)], rhs, ((0,), (0,))).astype(BF)

    far = chunk(2)
    fwd1[:half] = far[:half]
    bwd1[half:] = far[half:]
    right = chunk(1)
    fwd1[half:] = right[half:]
    fwd2[...] = right[:half]
    left = chunk(3)
    bwd1[:half] = left[:half]
    bwd2[...] = left[half:]
    own[...] = chunk(0)


def forward(raw_ref, up_ref, xs, ds, act, slope, hid, turn):
    groups = raw_ref.shape[0]
    from_tiles(raw_ref, 0, xs, groups, turn)
    from_tiles(raw_ref, 9, ds, groups, turn)
    hid[...] = matmul(xs[...], up_ref[0], ((1,), (0,)))
    step = 32

    def block(i, carry):
        at = pl.ds(pl.multiple_of(i * step, step), step)
        v = hid[at, :]
        cdf = 0.5 * (1.0 + lax.erf(v * 0.7071067811865476))
        pdf = jnp.exp(-0.5 * v * v) * 0.3989422804014327
        act[at, :] = (v * cdf).astype(BF)
        slope[at, :] = cdf + v * pdf
        return carry

    lax.fori_loop(0, hid.shape[0] // step, block, 0)


def expert_kernel(
    raw_ref, up_ref, up_turned, down_turned, ds_own, act_own, slope_own,
    fwd1, bwd1, fwd2, bwd2, own, xs, dh, keep, give,
    ds, act, slope, work, gate, half_ds, half_act, turn,
):
    groups = raw_ref.shape[0]
    rows = 9 * groups
    forward(raw_ref, up_ref, xs, half_ds, half_act, slope, work.at[:rows], turn)
    ds[:rows] = ds_own[...]
    ds[rows:] = half_ds[...]
    act[:rows] = act_own[...]
    act[rows:] = half_act[...]
    weight_parts(act, ds[...], lax.axis_index("dp"), fwd1, bwd1, fwd2, bwd2, own)
    work[...] = matmul(ds[...], down_turned[...], ((1,), (0,)))
    step = 32
    for half, slopes in enumerate((slope_own, slope)):

        def block(i, carry):
            here = pl.ds(pl.multiple_of(i * step, step), step)
            at = pl.ds(pl.multiple_of(half * rows + i * step, step), step)
            d = work[at, :]
            dh[at, :] = (d * slopes[here, :]).astype(BF)
            total = jnp.sum(act[at, :].astype(F32) * d, axis=1, keepdims=True)
            gate[at, :] = jnp.broadcast_to(total, (step, LANES))
            return carry

        lax.fori_loop(0, rows // step, block, 0)
    work[...] = matmul(dh[...], up_turned[...], ((1,), (0,)))
    lane = lax.broadcasted_iota(jnp.int32, (groups, 8, LANES), 2)
    for row, ref in ((0, keep), (rows, give)):
        to_tiles(work, row, ref, 0, groups, turn)
        last = gate[row + 8 * groups : row + rows, :]
        for j in range(8):
            turn[:, j, :] = last
        first = gate[row : row + 8 * groups, :].reshape(groups, 8, LANES)
        ref[:, 9] = jnp.where(lane < 64, first, turn[...]).astype(BF)


def up_kernel(xs_own, xs_other, dh, fwd1, bwd1, fwd2, bwd2, own, xs):
    rows = xs_own.shape[0]
    xs[:rows] = xs_own[...]
    xs[rows:] = xs_other[...]
    weight_parts(xs, dh[...], lax.axis_index("dp"), fwd1, bwd1, fwd2, bwd2, own)


def ring_kernel(fwd2, left, bwd2, right, fwd_out, bwd_out):
    half = fwd2.shape[0]
    fwd_out[...] = (fwd2[...].astype(F32) + left[:half].astype(F32)).astype(BF)
    bwd_out[...] = (bwd2[...].astype(F32) + right[half:].astype(F32)).astype(BF)


def final_kernel(own, left, right, left2, right2, out):
    half = left2.shape[0]
    low = own[:half].astype(F32) + right[:half].astype(F32)
    out[:half] = (low + left2[...].astype(F32)).astype(BF)
    high = own[half:].astype(F32) + left[half:].astype(F32)
    out[half:] = (high + right2[...].astype(F32)).astype(BF)


def unpack_kernel(back_ref, gate_ref, expert_ref, slot_ref, out_ref, gate_out_ref, rowbuf, turn):
    groups = back_ref.shape[0]
    count = out_ref.shape[0]
    from_tiles(back_ref, 0, rowbuf, groups, turn)
    expert = expert_ref[...].reshape(1, count)
    slot = slot_ref[...].reshape(1, count)
    rows = lax.broadcasted_iota(jnp.int32, (9 * groups, count), 0)
    pick = jnp.where(rows == slot_row(expert, slot, groups), 1.0, 0.0).astype(BF)
    out_ref[...] = matmul(pick, rowbuf[...], ((0,), (0,))).astype(BF)
    gates = back_ref[:, 9].astype(F32).reshape(8 * groups, LANES).astype(BF)
    rows = lax.broadcasted_iota(jnp.int32, (8 * groups, count), 0)
    low = jnp.where(rows == slot_row(expert, slot, groups), 1.0, 0.0).astype(BF)
    high = jnp.where((rows == expert * 8) & (slot == 8), 1.0, 0.0).astype(BF)
    low = matmul(gates, low, ((0,), (0,)))
    high = matmul(gates, high, ((0,), (0,)))
    total = low[0:1, :] + high[64:65, :]
    gate = gate_ref[...].astype(F32).reshape(1, count)
    gate_out_ref[...] = (total / gate).astype(BF).reshape(count)


def call(kernel, out, scratch, *args):
    whole = pl.BlockSpec(memory_space=pltpu.VMEM)
    return pl.pallas_call(
        kernel,
        out_shape=out,
        in_specs=[whole] * len(args),
        out_specs=jax.tree.map(lambda _: whole, out),
        scratch_shapes=scratch,
        compiler_params=pltpu.CompilerParams(vmem_limit_bytes=VMEM),
    )(*args)


def after(value, earlier):
    return lax.optimization_barrier((value, earlier))[0]


def shape(*dims, dtype=BF):
    return jax.ShapeDtypeStruct(dims, dtype)


AHEAD = [(i, (i + 1) % 4) for i in range(4)]
BEHIND = [(i, (i + 3) % 4) for i in range(4)]


def ring(fwd, bwd):
    return lax.ppermute(fwd, "dp", AHEAD), lax.ppermute(bwd, "dp", BEHIND)


def on_device(tokens_in, out_grad, gates, expert_ids, slot_ids, w_up, w_down):
    groups = lax.axis_size("chip")
    count, width = tokens_in.shape
    hidden = w_up.shape[2]
    rows = 9 * groups
    turn = pltpu.VMEM((groups, 8, LANES), F32)
    swap = [(0, 1), (1, 0)]

    def exchange(values):
        return lax.all_to_all(values, "chip", split_axis=0, concat_axis=0, tiled=True)

    def parts(length, columns):
        quarter = length // 4
        return (
            shape(quarter, columns),
            shape(quarter, columns),
            shape(quarter // 2, columns),
            shape(quarter // 2, columns),
            shape(quarter, columns),
        )

    sent = call(
        pack_kernel,
        shape(groups, 18, 8, LANES),
        [pltpu.VMEM((rows, width), F32), turn],
        tokens_in,
        out_grad,
        gates,
        expert_ids,
        slot_ids,
    )
    mine = exchange(sent)
    up_turned, down_turned = call(
        turn_kernel, (shape(hidden, width), shape(width, hidden)), [], w_up, w_down
    )
    mine, up_turned = lax.optimization_barrier((mine, up_turned))
    other = lax.ppermute(mine, "core", swap)
    half = (
        shape(rows, width),
        shape(rows, width),
        shape(rows, hidden),
        shape(rows, hidden, dtype=F32),
    )
    hid = pltpu.VMEM((rows, hidden), F32)
    xs_own, ds_own, act_own, slope_own = call(forward, half, [hid, turn], mine, w_up)
    returned = shape(groups, 10, 8, LANES)
    *down, xs_other, dh, keep, give = call(
        expert_kernel,
        parts(hidden, width) + (shape(rows, width), shape(2 * rows, hidden), returned, returned),
        [
            pltpu.VMEM((2 * rows, width), BF),
            pltpu.VMEM((2 * rows, hidden), BF),
            pltpu.VMEM((rows, hidden), F32),
            pltpu.VMEM((2 * rows, width), F32),
            pltpu.VMEM((2 * rows, LANES), F32),
            pltpu.VMEM((rows, width), BF),
            pltpu.VMEM((rows, hidden), BF),
            turn,
        ],
        other,
        w_up,
        up_turned,
        down_turned,
        ds_own,
        act_own,
        slope_own,
    )
    left_d, right_d = ring(down[0], down[1])
    got = lax.ppermute(give, "core", swap)
    both = (keep.astype(F32) + got.astype(F32)).astype(BF)
    back = exchange(both)
    pair = lambda parts: (shape(*parts[2].shape), shape(*parts[3].shape))
    down2 = call(ring_kernel, pair(down), [], down[2], left_d, down[3], right_d)
    xs_own = after(xs_own, down2)
    down2 = ring(*down2)
    up = call(
        up_kernel, parts(width, hidden), [pltpu.VMEM((2 * rows, width), BF)], xs_own, xs_other, dh
    )
    left_u, right_u = ring(up[0], up[1])
    down_grad = call(final_kernel, shape(hidden // 4, width), [], down[4], left_d, right_d, *down2)
    left_u, right_u, down_grad = lax.optimization_barrier((left_u, right_u, down_grad))
    up2 = ring(*call(ring_kernel, pair(up), [], up[2], left_u, up[3], right_u))
    in_grad, gate_grad = call(
        unpack_kernel,
        (shape(count, width), shape(count)),
        [pltpu.VMEM((rows, width), BF), turn],
        back,
        gates,
        expert_ids,
        slot_ids,
    )
    *up2, in_grad = lax.optimization_barrier((*up2, in_grad))
    up_grad = call(final_kernel, shape(width // 4, hidden), [], up[4], left_u, right_u, *up2)
    return (in_grad, gate_grad, up_grad[None], down_grad[None])


def solution(mesh):
    chips = mesh.devices.reshape(mesh.shape["expert"] // 2, 2, mesh.shape["dp"])
    finer = Mesh(chips, ("chip", "core", "dp"))
    tokens = ("chip", "core", "dp")
    pieces = ("chip", "core")
    return jax.shard_map(
        on_device,
        mesh=finer,
        in_specs=(
            P(tokens, None),
            P(tokens, None),
            P(tokens),
            P(tokens),
            P(tokens),
            P(pieces, None, None),
            P(pieces, None, None),
        ),
        out_specs=(
            P(tokens, None),
            P(tokens),
            P(pieces, "dp", None),
            P(pieces, "dp", None),
        ),
        check_vma=False,
    )
```

```python
import functools

import jax
import jax.numpy as jnp
from jax import lax
from jax.experimental import pallas as pl
from jax.experimental.pallas import tpu as pltpu
from jax.sharding import Mesh, PartitionSpec as P

BF = jnp.bfloat16
F32 = jnp.float32
VMEM = 56 * 1024 * 1024
LANES = 128


def matmul(a, b, contract):
    return lax.dot_general(a, b, (contract, ((), ())), preferred_element_type=F32)


def slot_row(expert, slot, groups):
    return jnp.where(slot < 8, expert * 8 + slot, 8 * groups + expert)


def to_tiles(get, out_ref, base, groups, turn):
    for j in range(8):
        part = get(0, 8 * groups, j)
        out_ref[:, base + j] = part.reshape(groups, 8, LANES).astype(BF)
        turn[:, j, :] = get(8 * groups, 9 * groups, j)
    out_ref[:, base + 8] = turn[...].astype(BF)


def from_tiles(ref, base, dst_ref, row, groups, turn):
    turn[...] = ref[:, base + 8].astype(F32)
    for j in range(8):
        cols = slice(LANES * j, LANES * (j + 1))
        part = ref[:, base + j].astype(F32).reshape(8 * groups, LANES)
        dst_ref[row : row + 8 * groups, cols] = part.astype(BF)
        dst_ref[row + 8 * groups : row + 9 * groups, cols] = turn[:, j, :].astype(BF)


def pack_kernel(x_ref, g_ref, gate_ref, expert_ref, slot_ref, out_ref, full, turn):
    groups = out_ref.shape[0]
    count = x_ref.shape[0]
    place = slot_row(expert_ref[...], slot_ref[...], groups).reshape(1, count)
    rows = lax.broadcasted_iota(jnp.int32, (9 * groups, count), 0)
    hit = rows == place
    gate = gate_ref[...].astype(F32).reshape(1, count)
    for side, (ref, scale) in enumerate(((x_ref, 1.0), (g_ref, gate))):
        pick = jnp.where(hit, scale, 0.0).astype(BF)
        full[...] = matmul(pick, ref[...], ((1,), (0,)))
        to_tiles(
            lambda a, b, j: full[a:b, LANES * j : LANES * (j + 1)],
            out_ref,
            9 * side,
            groups,
            turn,
        )


def weight_parts(lhs_ref, rhs, me, fwd1, bwd1, fwd2, bwd2, own):
    half = own.shape[0] // 2
    size = 2 * half

    def chunk(step):
        at = pl.multiple_of(lax.rem(me + step, 4) * size, size)
        return matmul(lhs_ref[:, pl.ds(at, size)], rhs, ((0,), (0,))).astype(BF)

    far = chunk(2)
    fwd1[:half] = far[:half]
    bwd1[half:] = far[half:]
    right = chunk(1)
    fwd1[half:] = right[half:]
    fwd2[...] = right[:half]
    left = chunk(3)
    bwd1[:half] = left[:half]
    bwd2[...] = left[half:]
    own[...] = chunk(0)


def unpacked(mine_ref, other_ref, xs, ds, turn):
    groups = mine_ref.shape[0]
    for part, ref in enumerate((mine_ref, other_ref)):
        from_tiles(ref, 0, xs, part * 9 * groups, groups, turn)
        from_tiles(ref, 9, ds, part * 9 * groups, groups, turn)


def activation(hid, dact, act, dh, gate):
    step = 32

    def block(i, carry):
        at = pl.ds(pl.multiple_of(i * step, step), step)
        v = hid[at, :]
        d = dact[at, :]
        cdf = 0.5 * (1.0 + lax.erf(v * 0.7071067811865476))
        pdf = jnp.exp(-0.5 * v * v) * 0.3989422804014327
        a = (v * cdf).astype(BF)
        act[at, :] = a
        dh[at, :] = (d * (cdf + v * pdf)).astype(BF)
        total = jnp.sum(a.astype(F32) * d, axis=1, keepdims=True)
        gate[at, :] = jnp.broadcast_to(total, (step, LANES))
        return carry

    lax.fori_loop(0, hid.shape[0] // step, block, 0)


def returned(dh, gate, up_ref, mine_ref, other_ref, full, turn):
    groups = mine_ref.shape[0]
    rows = 9 * groups
    full[...] = matmul(dh[...], up_ref[0], ((1,), (1,)))
    lane = lax.broadcasted_iota(jnp.int32, (groups, 8, LANES), 2)
    for part, ref in enumerate((mine_ref, other_ref)):
        at = part * rows
        to_tiles(
            lambda a, b, j: full[at + a : at + b, LANES * j : LANES * (j + 1)], ref, 0, groups, turn
        )
        last = gate[at + 8 * groups : at + rows, :]
        for j in range(8):
            turn[:, j, :] = last
        first = gate[at : at + 8 * groups, :].reshape(groups, 8, LANES)
        ref[:, 9] = jnp.where(lane < 64, first, turn[...]).astype(BF)


def expert_kernel(
    mine_ref, other_ref, up_ref, down_ref, xs, dh, keep, give, fwd1, bwd1, fwd2, bwd2, own, gate, ds, act, hid, dact, turn
):
    unpacked(mine_ref, other_ref, xs, ds, turn)
    hid[...] = matmul(xs[...], up_ref[0], ((1,), (0,)))
    dact[...] = matmul(ds[...], down_ref[0], ((1,), (1,)))
    activation(hid, dact, act, dh, gate)
    weight_parts(act, ds[...], lax.axis_index("dp"), fwd1, bwd1, fwd2, bwd2, own)
    returned(dh, gate, up_ref, keep, give, hid, turn)


def up_kernel(xs, dh, fwd1, bwd1, fwd2, bwd2, own):
    weight_parts(xs, dh[...], lax.axis_index("dp"), fwd1, bwd1, fwd2, bwd2, own)


def unpack_kernel(back_ref, gate_ref, expert_ref, slot_ref, out_ref, gate_out_ref, rowbuf, turn):
    groups = back_ref.shape[0]
    count = out_ref.shape[0]
    from_tiles(back_ref, 0, rowbuf, 0, groups, turn)
    expert = expert_ref[...].reshape(1, count)
    slot = slot_ref[...].reshape(1, count)
    rows = lax.broadcasted_iota(jnp.int32, (9 * groups, count), 0)
    pick = jnp.where(rows == slot_row(expert, slot, groups), 1.0, 0.0).astype(BF)
    out_ref[...] = matmul(pick, rowbuf[...], ((0,), (0,))).astype(BF)
    gates = back_ref[:, 9].astype(F32).reshape(8 * groups, LANES).astype(BF)
    rows = lax.broadcasted_iota(jnp.int32, (8 * groups, count), 0)
    low = jnp.where(rows == slot_row(expert, slot, groups), 1.0, 0.0).astype(BF)
    high = jnp.where((rows == expert * 8) & (slot == 8), 1.0, 0.0).astype(BF)
    low = matmul(gates, low, ((0,), (0,)))
    high = matmul(gates, high, ((0,), (0,)))
    total = low[0:1, :] + high[64:65, :]
    gate = gate_ref[...].astype(F32).reshape(1, count)
    gate_out_ref[...] = (total / gate).astype(BF).reshape(count)


def call(kernel, out, scratch, *args):
    whole = pl.BlockSpec(memory_space=pltpu.VMEM)
    return pl.pallas_call(
        kernel,
        out_shape=out,
        in_specs=[whole] * len(args),
        out_specs=jax.tree.map(lambda _: whole, out),
        scratch_shapes=scratch,
        compiler_params=pltpu.CompilerParams(vmem_limit_bytes=VMEM),
    )(*args)


def shape(*dims, dtype=BF):
    return jax.ShapeDtypeStruct(dims, dtype)


AHEAD = [(i, (i + 1) % 4) for i in range(4)]
BEHIND = [(i, (i + 3) % 4) for i in range(4)]


def ring(fwd, bwd):
    return lax.ppermute(fwd, "dp", AHEAD), lax.ppermute(bwd, "dp", BEHIND)


def second(parts, left, right):
    half = parts[2].shape[0]
    fwd = (parts[2].astype(F32) + left[:half].astype(F32)).astype(BF)
    bwd = (parts[3].astype(F32) + right[half:].astype(F32)).astype(BF)
    return fwd, bwd


def total(own, left, right, left2, right2):
    half, columns = left2.shape
    split = lambda a: a.reshape(2, half, columns)
    both = lambda a: jnp.broadcast_to(a[None], (2, half, columns))
    low = lax.broadcasted_iota(jnp.int32, (2, half, columns), 0) == 0
    first = jnp.where(low, split(right), split(left)).astype(F32)
    then = jnp.where(low, both(left2), both(right2)).astype(F32)
    return (split(own).astype(F32) + first + then).astype(BF).reshape(2 * half, columns)


def after(value, earlier):
    return lax.optimization_barrier((value, earlier))[0]


def on_device(tokens_in, out_grad, gates, expert_ids, slot_ids, w_up, w_down):
    groups = lax.axis_size("chip")
    count, width = tokens_in.shape
    hidden = w_up.shape[2]
    rows = 9 * groups
    turn = pltpu.VMEM((groups, 8, LANES), F32)
    swap = [(0, 1), (1, 0)]
    sent = call(
        pack_kernel,
        shape(groups, 18, 8, LANES),
        [pltpu.VMEM((rows, width), F32), turn],
        tokens_in,
        out_grad,
        gates,
        expert_ids,
        slot_ids,
    )
    mine = lax.all_to_all(sent, "chip", split_axis=0, concat_axis=0, tiled=True)
    other = lax.ppermute(mine, "core", swap)

    def parts(length, columns):
        quarter = length // 4
        return (
            shape(quarter, columns),
            shape(quarter, columns),
            shape(quarter // 2, columns),
            shape(quarter // 2, columns),
            shape(quarter, columns),
        )

    with jax.named_scope("expert_input"):
      xs, dh, keep, give, *down = call(
        expert_kernel,
        (shape(2 * rows, width), shape(2 * rows, hidden), shape(groups, 10, 8, LANES), shape(groups, 10, 8, LANES))
        + parts(hidden, width),
        [pltpu.VMEM((2 * rows, LANES), F32), pltpu.VMEM((2 * rows, width), BF),
            pltpu.VMEM((2 * rows, hidden), BF),
            pltpu.VMEM((2 * rows, hidden), F32),
            pltpu.VMEM((2 * rows, hidden), F32),
            turn,
        ],
        mine,
        other,
        w_up,
        w_down,
      )
    with jax.named_scope("swap_back"):
      got = lax.ppermute(give, "core", swap)
    both = (keep.astype(F32) + got.astype(F32)).astype(BF)
    with jax.named_scope("rows_back"):
      back = lax.all_to_all(both, "chip", split_axis=0, concat_axis=0, tiled=True)
    with jax.named_scope("unpack"):
      in_grad, gate_grad = call(
          unpack_kernel,
          (shape(count, width), shape(count)),
          [pltpu.VMEM((rows, width), BF), turn],
          back,
          gates,
          expert_ids,
          slot_ids,
      )
    with jax.named_scope("down_one"):
      left_d, right_d = ring(down[0], down[1])
    down2 = second(down, left_d, right_d)
    with jax.named_scope("down_two"):
      left_d2, right_d2 = ring(*down2)
    with jax.named_scope("up"):
      up = call(up_kernel, parts(width, hidden), [], xs, dh)
    down_grad = total(down[4], left_d, right_d, left_d2, right_d2)
    with jax.named_scope("up_one"):
      left_u, right_u = ring(up[0], up[1])
    up2 = second(up, left_u, right_u)
    with jax.named_scope("up_two"):
      left_u2, right_u2 = ring(*up2)
    left_u2, right_u2, down_grad = lax.optimization_barrier((left_u2, right_u2, down_grad))
    up_grad = total(up[4], left_u, right_u, left_u2, right_u2)
    return (in_grad, gate_grad, up_grad[None], down_grad[None])


def solution(mesh):
    chips = mesh.devices.reshape(mesh.shape["expert"] // 2, 2, mesh.shape["dp"])
    finer = Mesh(chips, ("chip", "core", "dp"))
    tokens = ("chip", "core", "dp")
    pieces = ("chip", "core")
    return jax.shard_map(
        on_device,
        mesh=finer,
        in_specs=(
            P(tokens, None),
            P(tokens, None),
            P(tokens),
            P(tokens),
            P(tokens),
            P(pieces, None, None),
            P(pieces, None, None),
        ),
        out_specs=(
            P(tokens, None),
            P(tokens),
            P(pieces, "dp", None),
            P(pieces, "dp", None),
        ),
        check_vma=False,
    )
```

```python
import functools

import jax
import jax.numpy as jnp
from jax import lax
from jax.experimental import pallas as pl
from jax.experimental.pallas import tpu as pltpu
from jax.sharding import Mesh, PartitionSpec as P

BF = jnp.bfloat16
F32 = jnp.float32
VMEM = 56 * 1024 * 1024
LANES = 128


def matmul(a, b, contract):
    return lax.dot_general(a, b, (contract, ((), ())), preferred_element_type=F32)


def slot_row(expert, slot, groups):
    return jnp.where(slot < 8, expert * 8 + slot, 8 * groups + expert)


def to_tiles(get, out_ref, base, groups, turn):
    for j in range(8):
        part = get(0, 8 * groups, j)
        out_ref[:, base + j] = part.reshape(groups, 8, LANES).astype(BF)
        turn[:, j, :] = get(8 * groups, 9 * groups, j)
    out_ref[:, base + 8] = turn[...].astype(BF)


def from_tiles(ref, base, dst_ref, row, groups, turn):
    turn[...] = ref[:, base + 8].astype(F32)
    for j in range(8):
        cols = slice(LANES * j, LANES * (j + 1))
        part = ref[:, base + j].astype(F32).reshape(8 * groups, LANES)
        dst_ref[row : row + 8 * groups, cols] = part.astype(BF)
        dst_ref[row + 8 * groups : row + 9 * groups, cols] = turn[:, j, :].astype(BF)


def pack_kernel(x_ref, g_ref, gate_ref, expert_ref, slot_ref, out_ref, full, turn):
    groups = out_ref.shape[0]
    count = x_ref.shape[0]
    place = slot_row(expert_ref[...], slot_ref[...], groups).reshape(1, count)
    rows = lax.broadcasted_iota(jnp.int32, (9 * groups, count), 0)
    hit = rows == place
    gate = gate_ref[...].astype(F32).reshape(1, count)
    for side, (ref, scale) in enumerate(((x_ref, 1.0), (g_ref, gate))):
        pick = jnp.where(hit, scale, 0.0).astype(BF)
        full[...] = matmul(pick, ref[...], ((1,), (0,)))
        to_tiles(
            lambda a, b, j: full[a:b, LANES * j : LANES * (j + 1)],
            out_ref,
            9 * side,
            groups,
            turn,
        )


def weight_parts(lhs_ref, rhs, me, fwd1, bwd1, fwd2, bwd2, own, held, sems):
    half = own.shape[0] // 2
    size = 2 * half
    low, high = pl.ds(0, half), pl.ds(half, half)
    both = pl.ds(0, size)
    places = (
        (2, ((low, fwd1.at[low]), (high, bwd1.at[high]))),
        (1, ((high, fwd1.at[high]), (low, fwd2))),
        (3, ((low, bwd1.at[low]), (high, bwd2))),
        (0, ((both, own),)),
    )
    copies = []
    for step, targets in places:
        at = pl.multiple_of(lax.rem(me + step, 4) * size, size)
        held[step] = matmul(lhs_ref[:, pl.ds(at, size)], rhs, ((0,), (0,))).astype(BF)
        for rows, target in targets:
            copy = pltpu.make_async_copy(held.at[step, rows], target, sems.at[len(copies)])
            copy.start()
            copies.append(copy)
    return copies


def activation(hid, dact, act, dh, gate):
    step = 32

    def block(i, carry):
        at = pl.ds(pl.multiple_of(i * step, step), step)
        v = hid[at, :]
        d = dact[at, :]
        cdf = 0.5 * (1.0 + lax.erf(v * 0.7071067811865476))
        pdf = jnp.exp(-0.5 * v * v) * 0.3989422804014327
        a = (v * cdf).astype(BF)
        act[at, :] = a
        dh[at, :] = (d * (cdf + v * pdf)).astype(BF)
        total = jnp.sum(a.astype(F32) * d, axis=1, keepdims=True)
        gate[at, :] = jnp.broadcast_to(total, (step, LANES))
        return carry

    lax.fori_loop(0, hid.shape[0] // step, block, 0)


def returned(dh, gate, up_ref, mine_ref, other_ref, full, turn):
    groups = mine_ref.shape[0]
    rows = 9 * groups
    full[...] = matmul(dh[...], up_ref[0], ((1,), (1,)))
    lane = lax.broadcasted_iota(jnp.int32, (groups, 8, LANES), 2)
    for part, ref in enumerate((mine_ref, other_ref)):
        at = part * rows
        to_tiles(
            lambda a, b, j: full[at + a : at + b, LANES * j : LANES * (j + 1)], ref, 0, groups, turn
        )
        last = gate[at + 8 * groups : at + rows, :]
        for j in range(8):
            turn[:, j, :] = last
        first = gate[at : at + 8 * groups, :].reshape(groups, 8, LANES)
        ref[:, 9] = jnp.where(lane < 64, first, turn[...]).astype(BF)


def expert_kernel(
    mine_ref, other_hbm, up_hbm, down_hbm,
    xs, dh, keep, give, fwd1, bwd1, fwd2, bwd2, own,
    gate, ds, act, hid, dact, turn, other_ref, up_ref, down_ref, held, out_sems, in_sems,
):
    loads = [
        pltpu.make_async_copy(source, target, in_sems.at[n])
        for n, (source, target) in enumerate(
            ((other_hbm, other_ref), (up_hbm, up_ref), (down_hbm, down_ref))
        )
    ]
    for load in loads:
        load.start()
    groups = mine_ref.shape[0]
    rows = 9 * groups
    from_tiles(mine_ref, 0, xs, 0, groups, turn)
    from_tiles(mine_ref, 9, ds, 0, groups, turn)
    loads[0].wait()
    from_tiles(other_ref, 0, xs, rows, groups, turn)
    from_tiles(other_ref, 9, ds, rows, groups, turn)
    loads[1].wait()
    hid[...] = matmul(xs[...], up_ref[0], ((1,), (0,)))
    loads[2].wait()
    dact[...] = matmul(ds[...], down_ref[0], ((1,), (1,)))
    activation(hid, dact, act, dh, gate)
    me = lax.axis_index("dp")
    stores = weight_parts(act, ds[...], me, fwd1, bwd1, fwd2, bwd2, own, held, out_sems)
    returned(dh, gate, up_ref, keep, give, hid, turn)
    for store in stores:
        store.wait()


def up_kernel(xs, dh, fwd1, bwd1, fwd2, bwd2, own, held, out_sems):
    me = lax.axis_index("dp")
    for store in weight_parts(xs, dh[...], me, fwd1, bwd1, fwd2, bwd2, own, held, out_sems):
        store.wait()


def unpack_kernel(back_ref, gate_ref, expert_ref, slot_ref, out_ref, gate_out_ref, rowbuf, turn):
    groups = back_ref.shape[0]
    count = out_ref.shape[0]
    from_tiles(back_ref, 0, rowbuf, 0, groups, turn)
    expert = expert_ref[...].reshape(1, count)
    slot = slot_ref[...].reshape(1, count)
    rows = lax.broadcasted_iota(jnp.int32, (9 * groups, count), 0)
    pick = jnp.where(rows == slot_row(expert, slot, groups), 1.0, 0.0).astype(BF)
    out_ref[...] = matmul(pick, rowbuf[...], ((0,), (0,))).astype(BF)
    gates = back_ref[:, 9].astype(F32).reshape(8 * groups, LANES).astype(BF)
    rows = lax.broadcasted_iota(jnp.int32, (8 * groups, count), 0)
    low = jnp.where(rows == slot_row(expert, slot, groups), 1.0, 0.0).astype(BF)
    high = jnp.where((rows == expert * 8) & (slot == 8), 1.0, 0.0).astype(BF)
    low = matmul(gates, low, ((0,), (0,)))
    high = matmul(gates, high, ((0,), (0,)))
    total = low[0:1, :] + high[64:65, :]
    gate = gate_ref[...].astype(F32).reshape(1, count)
    gate_out_ref[...] = (total / gate).astype(BF).reshape(count)


def call(kernel, out, scratch, *args, far_in=(), far_out=()):
    near = pl.BlockSpec(memory_space=pltpu.VMEM)
    far = pl.BlockSpec(memory_space=pltpu.HBM)
    several = isinstance(out, tuple)
    count = len(out) if several else 1
    specs = tuple(far if n in far_out else near for n in range(count))
    return pl.pallas_call(
        kernel,
        out_shape=out,
        in_specs=[far if n in far_in else near for n in range(len(args))],
        out_specs=specs if several else near,
        scratch_shapes=scratch,
        compiler_params=pltpu.CompilerParams(vmem_limit_bytes=VMEM),
    )(*args)


def shape(*dims, dtype=BF):
    return jax.ShapeDtypeStruct(dims, dtype)


AHEAD = [(i, (i + 1) % 4) for i in range(4)]
BEHIND = [(i, (i + 3) % 4) for i in range(4)]


def ring(fwd, bwd):
    return lax.ppermute(fwd, "dp", AHEAD), lax.ppermute(bwd, "dp", BEHIND)


def second(parts, left, right):
    half = parts[2].shape[0]
    fwd = (parts[2].astype(F32) + left[:half].astype(F32)).astype(BF)
    bwd = (parts[3].astype(F32) + right[half:].astype(F32)).astype(BF)
    return fwd, bwd


def total(own, left, right, left2, right2):
    half, columns = left2.shape
    split = lambda a: a.reshape(2, half, columns)
    both = lambda a: jnp.broadcast_to(a[None], (2, half, columns))
    low = lax.broadcasted_iota(jnp.int32, (2, half, columns), 0) == 0
    first = jnp.where(low, split(right), split(left)).astype(F32)
    then = jnp.where(low, both(left2), both(right2)).astype(F32)
    return (split(own).astype(F32) + first + then).astype(BF).reshape(2 * half, columns)


def after(value, earlier):
    return lax.optimization_barrier((value, earlier))[0]


def on_device(tokens_in, out_grad, gates, expert_ids, slot_ids, w_up, w_down):
    groups = lax.axis_size("chip")
    count, width = tokens_in.shape
    hidden = w_up.shape[2]
    rows = 9 * groups
    turn = pltpu.VMEM((groups, 8, LANES), F32)
    swap = [(0, 1), (1, 0)]
    sent = call(
        pack_kernel,
        shape(groups, 18, 8, LANES),
        [pltpu.VMEM((rows, width), F32), turn],
        tokens_in,
        out_grad,
        gates,
        expert_ids,
        slot_ids,
    )
    mine = lax.all_to_all(sent, "chip", split_axis=0, concat_axis=0, tiled=True)
    other = lax.ppermute(mine, "core", swap)

    def parts(length, columns):
        quarter = length // 4
        return (
            shape(quarter, columns),
            shape(quarter, columns),
            shape(quarter // 2, columns),
            shape(quarter // 2, columns),
            shape(quarter, columns),
        )

    held = pltpu.VMEM((4, hidden // 4, width), BF)
    out_sems = pltpu.SemaphoreType.DMA((7,))
    with jax.named_scope("expert_input"):
        xs, dh, keep, give, *down = call(
            expert_kernel,
            (
                shape(2 * rows, width),
                shape(2 * rows, hidden),
                shape(groups, 10, 8, LANES),
                shape(groups, 10, 8, LANES),
            )
            + parts(hidden, width),
            [
                pltpu.VMEM((2 * rows, LANES), F32),
                pltpu.VMEM((2 * rows, width), BF),
                pltpu.VMEM((2 * rows, hidden), BF),
                pltpu.VMEM((2 * rows, hidden), F32),
                pltpu.VMEM((2 * rows, hidden), F32),
                turn,
                pltpu.VMEM((groups, 18, 8, LANES), BF),
                pltpu.VMEM((1, width, hidden), BF),
                pltpu.VMEM((1, hidden, width), BF),
                held,
                out_sems,
                pltpu.SemaphoreType.DMA((3,)),
            ],
            mine,
            other,
            w_up,
            w_down,
            far_in=(1, 2, 3),
            far_out=(4, 5, 6, 7, 8),
        )
    with jax.named_scope("down_one"):
      left_d, right_d = ring(down[0], down[1])
    with jax.named_scope("swap_back"):
      got = lax.ppermute(give, "core", swap)
    with jax.named_scope("up"):
      up = call(
            up_kernel,
            parts(width, hidden),
            [pltpu.VMEM((4, width // 4, hidden), BF), out_sems],
            xs,
            dh,
            far_out=(0, 1, 2, 3, 4),
        )
    with jax.named_scope("up_one"):
      left_u, right_u = ring(up[0], up[1])
    both = (keep.astype(F32) + got.astype(F32)).astype(BF)
    with jax.named_scope("rows_back"):
      back = lax.all_to_all(both, "chip", split_axis=0, concat_axis=0, tiled=True)
    down2 = second(down, left_d, right_d)
    with jax.named_scope("down_two"):
      left_d2, right_d2 = ring(*down2)
    up2 = second(up, left_u, right_u)
    with jax.named_scope("up_two"):
      left_u2, right_u2 = ring(*up2)
    down_grad = total(down[4], left_d, right_d, left_d2, right_d2)
    with jax.named_scope("unpack"):
      in_grad, gate_grad = call(
          unpack_kernel,
          (shape(count, width), shape(count)),
          [pltpu.VMEM((rows, width), BF), turn],
          back,
          gates,
          expert_ids,
          slot_ids,
      )
    left_u2, right_u2, in_grad = lax.optimization_barrier((left_u2, right_u2, in_grad))
    left_u2, right_u2, down_grad = lax.optimization_barrier((left_u2, right_u2, down_grad))
    up_grad = total(up[4], left_u, right_u, left_u2, right_u2)
    return (in_grad, gate_grad, up_grad[None], down_grad[None])


def solution(mesh):
    chips = mesh.devices.reshape(mesh.shape["expert"] // 2, 2, mesh.shape["dp"])
    finer = Mesh(chips, ("chip", "core", "dp"))
    tokens = ("chip", "core", "dp")
    pieces = ("chip", "core")
    return jax.shard_map(
        on_device,
        mesh=finer,
        in_specs=(
            P(tokens, None),
            P(tokens, None),
            P(tokens),
            P(tokens),
            P(tokens),
            P(pieces, None, None),
            P(pieces, None, None),
        ),
        out_specs=(
            P(tokens, None),
            P(tokens),
            P(pieces, "dp", None),
            P(pieces, "dp", None),
        ),
        check_vma=False,
    )
```

```python
import functools

import jax
import jax.numpy as jnp
from jax import lax
from jax.experimental import pallas as pl
from jax.experimental.pallas import tpu as pltpu
from jax.sharding import Mesh, PartitionSpec as P

BF = jnp.bfloat16
F32 = jnp.float32
VMEM = 56 * 1024 * 1024
LANES = 128


def matmul(a, b, contract):
    return lax.dot_general(a, b, (contract, ((), ())), preferred_element_type=F32)


def slot_row(expert, slot, groups):
    return jnp.where(slot < 8, expert * 8 + slot, 8 * groups + expert)


def to_tiles(get, out_ref, base, groups, turn):
    for j in range(8):
        part = get(0, 8 * groups, j)
        out_ref[:, base + j] = part.reshape(groups, 8, LANES).astype(BF)
        turn[:, j, :] = get(8 * groups, 9 * groups, j)
    out_ref[:, base + 8] = turn[...].astype(BF)


def from_tiles(ref, base, dst_ref, row, groups, turn):
    turn[...] = ref[:, base + 8].astype(F32)
    for j in range(8):
        cols = slice(LANES * j, LANES * (j + 1))
        part = ref[:, base + j].astype(F32).reshape(8 * groups, LANES)
        dst_ref[row : row + 8 * groups, cols] = part.astype(BF)
        dst_ref[row + 8 * groups : row + 9 * groups, cols] = turn[:, j, :].astype(BF)


def pack_kernel(x_ref, g_ref, gate_ref, expert_ref, slot_ref, out_ref, full, turn):
    groups = out_ref.shape[0]
    count = x_ref.shape[0]
    place = slot_row(expert_ref[...], slot_ref[...], groups).reshape(1, count)
    rows = lax.broadcasted_iota(jnp.int32, (9 * groups, count), 0)
    hit = rows == place
    gate = gate_ref[...].astype(F32).reshape(1, count)
    for side, (ref, scale) in enumerate(((x_ref, 1.0), (g_ref, gate))):
        pick = jnp.where(hit, scale, 0.0).astype(BF)
        full[...] = matmul(pick, ref[...], ((1,), (0,)))
        to_tiles(
            lambda a, b, j: full[a:b, LANES * j : LANES * (j + 1)],
            out_ref,
            9 * side,
            groups,
            turn,
        )


def weight_parts(lhs_ref, rhs, me, fwd1, bwd1, fwd2, bwd2, own):
    half = own.shape[0] // 2
    size = 2 * half

    def chunk(step):
        at = pl.multiple_of(lax.rem(me + step, 4) * size, size)
        return matmul(lhs_ref[:, pl.ds(at, size)], rhs, ((0,), (0,))).astype(BF)

    far = chunk(2)
    fwd1[:half] = far[:half]
    bwd1[half:] = far[half:]
    right = chunk(1)
    fwd1[half:] = right[half:]
    fwd2[...] = right[:half]
    left = chunk(3)
    bwd1[:half] = left[:half]
    bwd2[...] = left[half:]
    own[...] = chunk(0)


def unpacked(mine_ref, other_ref, xs, ds, turn):
    groups = mine_ref.shape[0]
    for part, ref in enumerate((mine_ref, other_ref)):
        from_tiles(ref, 0, xs, part * 9 * groups, groups, turn)
        from_tiles(ref, 9, ds, part * 9 * groups, groups, turn)


def activation(hid, dact, act, dh, gate):
    step = 64

    def block(i, carry):
        at = pl.ds(pl.multiple_of(i * step, step), step)
        total = None
        for start in range(0, hid.shape[1], LANES):
            cols = pl.ds(start, LANES)
            v = hid[at, cols]
            d = dact[at, cols]
            cdf = 0.5 * (1.0 + lax.erf(v * 0.7071067811865476))
            pdf = jnp.exp(-0.5 * v * v) * 0.3989422804014327
            a = (v * cdf).astype(BF)
            act[at, cols] = a
            dh[at, cols] = (d * (cdf + v * pdf)).astype(BF)
            part = a.astype(F32) * d
            total = part if total is None else total + part
        row = jnp.sum(total, axis=1, keepdims=True)
        gate[at, :] = jnp.broadcast_to(row, (step, LANES))
        return carry

    lax.fori_loop(0, hid.shape[0] // step, block, 0)


def returned(dh, gate, up_ref, mine_ref, other_ref, full, turn):
    groups = mine_ref.shape[0]
    rows = 9 * groups
    full[...] = matmul(dh[...], up_ref[0], ((1,), (1,)))
    lane = lax.broadcasted_iota(jnp.int32, (groups, 8, LANES), 2)
    for part, ref in enumerate((mine_ref, other_ref)):
        at = part * rows
        to_tiles(
            lambda a, b, j: full[at + a : at + b, LANES * j : LANES * (j + 1)], ref, 0, groups, turn
        )
        last = gate[at + 8 * groups : at + rows, :]
        for j in range(8):
            turn[:, j, :] = last
        first = gate[at : at + 8 * groups, :].reshape(groups, 8, LANES)
        ref[:, 9] = jnp.where(lane < 64, first, turn[...]).astype(BF)


def expert_kernel(
    mine_ref, other_ref, up_ref, down_ref, xs, dh, keep, give, fwd1, bwd1, fwd2, bwd2, own, gate, ds, act, hid, dact, turn
):
    unpacked(mine_ref, other_ref, xs, ds, turn)
    hid[...] = matmul(xs[...], up_ref[0], ((1,), (0,)))
    dact[...] = matmul(ds[...], down_ref[0], ((1,), (1,)))
    activation(hid, dact, act, dh, gate)
    weight_parts(act, ds[...], lax.axis_index("dp"), fwd1, bwd1, fwd2, bwd2, own)
    returned(dh, gate, up_ref, keep, give, hid, turn)


def up_kernel(xs, dh, fwd1, bwd1, fwd2, bwd2, own):
    weight_parts(xs, dh[...], lax.axis_index("dp"), fwd1, bwd1, fwd2, bwd2, own)


def unpack_kernel(back_ref, gate_ref, expert_ref, slot_ref, out_ref, gate_out_ref, rowbuf, turn):
    groups = back_ref.shape[0]
    count = out_ref.shape[0]
    from_tiles(back_ref, 0, rowbuf, 0, groups, turn)
    expert = expert_ref[...].reshape(1, count)
    slot = slot_ref[...].reshape(1, count)
    rows = lax.broadcasted_iota(jnp.int32, (9 * groups, count), 0)
    pick = jnp.where(rows == slot_row(expert, slot, groups), 1.0, 0.0).astype(BF)
    out_ref[...] = matmul(pick, rowbuf[...], ((0,), (0,))).astype(BF)
    gates = back_ref[:, 9].astype(F32).reshape(8 * groups, LANES).astype(BF)
    rows = lax.broadcasted_iota(jnp.int32, (8 * groups, count), 0)
    low = jnp.where(rows == slot_row(expert, slot, groups), 1.0, 0.0).astype(BF)
    high = jnp.where((rows == expert * 8) & (slot == 8), 1.0, 0.0).astype(BF)
    low = matmul(gates, low, ((0,), (0,)))
    high = matmul(gates, high, ((0,), (0,)))
    total = low[0:1, :] + high[64:65, :]
    gate = gate_ref[...].astype(F32).reshape(1, count)
    gate_out_ref[...] = (total / gate).astype(BF).reshape(count)


def call(kernel, out, scratch, *args):
    whole = pl.BlockSpec(memory_space=pltpu.VMEM)
    return pl.pallas_call(
        kernel,
        out_shape=out,
        in_specs=[whole] * len(args),
        out_specs=jax.tree.map(lambda _: whole, out),
        scratch_shapes=scratch,
        compiler_params=pltpu.CompilerParams(vmem_limit_bytes=VMEM),
    )(*args)


def shape(*dims, dtype=BF):
    return jax.ShapeDtypeStruct(dims, dtype)


AHEAD = [(i, (i + 1) % 4) for i in range(4)]
BEHIND = [(i, (i + 3) % 4) for i in range(4)]


def ring(fwd, bwd):
    return lax.ppermute(fwd, "dp", AHEAD), lax.ppermute(bwd, "dp", BEHIND)


def second(parts, left, right):
    half = parts[2].shape[0]
    fwd = (parts[2].astype(F32) + left[:half].astype(F32)).astype(BF)
    bwd = (parts[3].astype(F32) + right[half:].astype(F32)).astype(BF)
    return fwd, bwd


def early(own, left, right):
    low = lax.broadcasted_iota(jnp.int32, own.shape, 0) < own.shape[0] // 2
    return lax.optimization_barrier(own.astype(F32) + jnp.where(low, right, left).astype(F32))


def total(begun, left2, right2):
    half, columns = left2.shape
    both = lambda a: jnp.broadcast_to(a[None], (2, half, columns))
    low = lax.broadcasted_iota(jnp.int32, (2, half, columns), 0) == 0
    then = jnp.where(low, both(left2), both(right2)).astype(F32)
    return (begun.reshape(2, half, columns) + then).astype(BF).reshape(2 * half, columns)


def after(value, earlier):
    return lax.optimization_barrier((value, earlier))[0]


def on_device(tokens_in, out_grad, gates, expert_ids, slot_ids, w_up, w_down):
    groups = lax.axis_size("chip")
    count, width = tokens_in.shape
    hidden = w_up.shape[2]
    rows = 9 * groups
    turn = pltpu.VMEM((groups, 8, LANES), F32)
    swap = [(0, 1), (1, 0)]
    sent = call(
        pack_kernel,
        shape(groups, 18, 8, LANES),
        [pltpu.VMEM((rows, width), F32), turn],
        tokens_in,
        out_grad,
        gates,
        expert_ids,
        slot_ids,
    )
    mine = lax.all_to_all(sent, "chip", split_axis=0, concat_axis=0, tiled=True)
    other = lax.ppermute(mine, "core", swap)

    def parts(length, columns):
        quarter = length // 4
        return (
            shape(quarter, columns),
            shape(quarter, columns),
            shape(quarter // 2, columns),
            shape(quarter // 2, columns),
            shape(quarter, columns),
        )

    with jax.named_scope("expert_input"):
      xs, dh, keep, give, *down = call(
        expert_kernel,
        (shape(2 * rows, width), shape(2 * rows, hidden), shape(groups, 10, 8, LANES), shape(groups, 10, 8, LANES))
        + parts(hidden, width),
        [pltpu.VMEM((2 * rows, LANES), F32), pltpu.VMEM((2 * rows, width), BF),
            pltpu.VMEM((2 * rows, hidden), BF),
            pltpu.VMEM((2 * rows, hidden), F32),
            pltpu.VMEM((2 * rows, hidden), F32),
            turn,
        ],
        mine,
        other,
        w_up,
        w_down,
      )
    with jax.named_scope("down_one"):
      left_d, right_d = ring(down[0], down[1])
    with jax.named_scope("swap_back"):
      got = lax.ppermute(give, "core", swap)
    with jax.named_scope("up"):
      up = call(up_kernel, parts(width, hidden), [], xs, dh)
    with jax.named_scope("up_one"):
      left_u, right_u = ring(up[0], up[1])
    both = (keep.astype(F32) + got.astype(F32)).astype(BF)
    with jax.named_scope("rows_back"):
      back = lax.all_to_all(both, "chip", split_axis=0, concat_axis=0, tiled=True)
    down2 = second(down, left_d, right_d)
    with jax.named_scope("down_two"):
      left_d2, right_d2 = ring(*down2)
    up2 = second(up, left_u, right_u)
    with jax.named_scope("up_two"):
      left_u2, right_u2 = ring(*up2)
    down_grad = total(early(down[4], left_d, right_d), left_d2, right_d2)
    with jax.named_scope("unpack"):
      in_grad, gate_grad = call(
          unpack_kernel,
          (shape(count, width), shape(count)),
          [pltpu.VMEM((rows, width), BF), turn],
          back,
          gates,
          expert_ids,
          slot_ids,
      )
    left_u2, right_u2, in_grad = lax.optimization_barrier((left_u2, right_u2, in_grad))
    left_u2, right_u2, down_grad = lax.optimization_barrier((left_u2, right_u2, down_grad))
    up_grad = total(early(up[4], left_u, right_u), left_u2, right_u2)
    return (in_grad, gate_grad, up_grad[None], down_grad[None])


def solution(mesh):
    chips = mesh.devices.reshape(mesh.shape["expert"] // 2, 2, mesh.shape["dp"])
    finer = Mesh(chips, ("chip", "core", "dp"))
    tokens = ("chip", "core", "dp")
    pieces = ("chip", "core")
    return jax.shard_map(
        on_device,
        mesh=finer,
        in_specs=(
            P(tokens, None),
            P(tokens, None),
            P(tokens),
            P(tokens),
            P(tokens),
            P(pieces, None, None),
            P(pieces, None, None),
        ),
        out_specs=(
            P(tokens, None),
            P(tokens),
            P(pieces, "dp", None),
            P(pieces, "dp", None),
        ),
        check_vma=False,
    )
```

```python
import functools

import jax
import jax.numpy as jnp
from jax import lax
from jax.experimental import pallas as pl
from jax.experimental.pallas import tpu as pltpu
from jax.sharding import Mesh, PartitionSpec as P

BF = jnp.bfloat16
F32 = jnp.float32
VMEM = 56 * 1024 * 1024
LANES = 128


def matmul(a, b, contract):
    return lax.dot_general(a, b, (contract, ((), ())), preferred_element_type=F32)


def slot_row(expert, slot, groups):
    return jnp.where(slot < 8, expert * 8 + slot, 8 * groups + expert)


def to_tiles(get, out_ref, base, groups, turn):
    for j in range(8):
        part = get(0, 8 * groups, j)
        out_ref[:, base + j] = part.reshape(groups, 8, LANES).astype(BF)
        turn[:, j, :] = get(8 * groups, 9 * groups, j)
    out_ref[:, base + 8] = turn[...].astype(BF)


def from_tiles(ref, base, dst_ref, row, groups, turn):
    turn[...] = ref[:, base + 8].astype(F32)
    for j in range(8):
        cols = slice(LANES * j, LANES * (j + 1))
        part = ref[:, base + j].astype(F32).reshape(8 * groups, LANES)
        dst_ref[row : row + 8 * groups, cols] = part.astype(BF)
        dst_ref[row + 8 * groups : row + 9 * groups, cols] = turn[:, j, :].astype(BF)


def pack_kernel(x_ref, g_ref, gate_ref, expert_ref, slot_ref, out_ref, full, turn):
    groups = out_ref.shape[0]
    count = x_ref.shape[0]
    place = slot_row(expert_ref[...], slot_ref[...], groups).reshape(1, count)
    rows = lax.broadcasted_iota(jnp.int32, (9 * groups, count), 0)
    hit = rows == place
    gate = gate_ref[...].astype(F32).reshape(1, count)
    for side, (ref, scale) in enumerate(((x_ref, 1.0), (g_ref, gate))):
        pick = jnp.where(hit, scale, 0.0).astype(BF)
        full[...] = matmul(pick, ref[...], ((1,), (0,)))
        to_tiles(
            lambda a, b, j: full[a:b, LANES * j : LANES * (j + 1)],
            out_ref,
            9 * side,
            groups,
            turn,
        )


def weight_parts(lhs_ref, rhs, me, fwd1, bwd1, fwd2, bwd2, own):
    half = own.shape[0] // 2
    size = 2 * half

    def chunk(step):
        at = pl.multiple_of(lax.rem(me + step, 4) * size, size)
        return matmul(lhs_ref[:, pl.ds(at, size)], rhs, ((0,), (0,))).astype(BF)

    far = chunk(2)
    fwd1[:half] = far[:half]
    bwd1[half:] = far[half:]
    right = chunk(1)
    fwd1[half:] = right[half:]
    fwd2[...] = right[:half]
    left = chunk(3)
    bwd1[:half] = left[:half]
    bwd2[...] = left[half:]
    own[...] = chunk(0)


def unpacked(mine_ref, other_ref, xs, ds, turn):
    groups = mine_ref.shape[0]
    for part, ref in enumerate((mine_ref, other_ref)):
        from_tiles(ref, 0, xs, part * 9 * groups, groups, turn)
        from_tiles(ref, 9, ds, part * 9 * groups, groups, turn)


def activation(hid, dact, act, dh, gate):
    step = 64

    def block(i, carry):
        at = pl.ds(pl.multiple_of(i * step, step), step)
        total = None
        for start in range(0, hid.shape[1], LANES):
            cols = pl.ds(start, LANES)
            v = hid[at, cols]
            d = dact[at, cols]
            cdf = 0.5 * (1.0 + lax.erf(v * 0.7071067811865476))
            pdf = jnp.exp(-0.5 * v * v) * 0.3989422804014327
            a = (v * cdf).astype(BF)
            act[at, cols] = a
            dh[at, cols] = (d * (cdf + v * pdf)).astype(BF)
            part = a.astype(F32) * d
            total = part if total is None else total + part
        row = jnp.sum(total, axis=1, keepdims=True)
        gate[at, :] = jnp.broadcast_to(row, (step, LANES))
        return carry

    lax.fori_loop(0, hid.shape[0] // step, block, 0)


def returned(dh, gate, up_ref, mine_ref, other_ref, full, turn):
    groups = mine_ref.shape[0]
    rows = 9 * groups
    full[...] = matmul(dh[...], up_ref[0], ((1,), (1,)))
    lane = lax.broadcasted_iota(jnp.int32, (groups, 8, LANES), 2)
    for part, ref in enumerate((mine_ref, other_ref)):
        at = part * rows
        to_tiles(
            lambda a, b, j: full[at + a : at + b, LANES * j : LANES * (j + 1)], ref, 0, groups, turn
        )
        last = gate[at + 8 * groups : at + rows, :]
        for j in range(8):
            turn[:, j, :] = last
        first = gate[at : at + 8 * groups, :].reshape(groups, 8, LANES)
        ref[:, 9] = jnp.where(lane < 64, first, turn[...]).astype(BF)


def expert_kernel(
    mine_ref, other_ref, up_ref, down_ref, keep, give, fwd1, bwd1, fwd2, bwd2, own, ufwd1, ubwd1, ufwd2, ubwd2, uown, xs, dh, gate, ds, act, hid, dact, turn
):
    unpacked(mine_ref, other_ref, xs, ds, turn)
    hid[...] = matmul(xs[...], up_ref[0], ((1,), (0,)))
    dact[...] = matmul(ds[...], down_ref[0], ((1,), (1,)))
    activation(hid, dact, act, dh, gate)
    weight_parts(act, ds[...], lax.axis_index("dp"), fwd1, bwd1, fwd2, bwd2, own)
    weight_parts(xs, dh[...], lax.axis_index("dp"), ufwd1, ubwd1, ufwd2, ubwd2, uown)
    returned(dh, gate, up_ref, keep, give, hid, turn)


def unpack_kernel(back_ref, gate_ref, expert_ref, slot_ref, out_ref, gate_out_ref, rowbuf, turn):
    groups = back_ref.shape[0]
    count = out_ref.shape[0]
    from_tiles(back_ref, 0, rowbuf, 0, groups, turn)
    expert = expert_ref[...].reshape(1, count)
    slot = slot_ref[...].reshape(1, count)
    rows = lax.broadcasted_iota(jnp.int32, (9 * groups, count), 0)
    pick = jnp.where(rows == slot_row(expert, slot, groups), 1.0, 0.0).astype(BF)
    out_ref[...] = matmul(pick, rowbuf[...], ((0,), (0,))).astype(BF)
    gates = back_ref[:, 9].astype(F32).reshape(8 * groups, LANES).astype(BF)
    rows = lax.broadcasted_iota(jnp.int32, (8 * groups, count), 0)
    low = jnp.where(rows == slot_row(expert, slot, groups), 1.0, 0.0).astype(BF)
    high = jnp.where((rows == expert * 8) & (slot == 8), 1.0, 0.0).astype(BF)
    low = matmul(gates, low, ((0,), (0,)))
    high = matmul(gates, high, ((0,), (0,)))
    total = low[0:1, :] + high[64:65, :]
    gate = gate_ref[...].astype(F32).reshape(1, count)
    gate_out_ref[...] = (total / gate).astype(BF).reshape(count)


def call(kernel, out, scratch, *args):
    whole = pl.BlockSpec(memory_space=pltpu.VMEM)
    return pl.pallas_call(
        kernel,
        out_shape=out,
        in_specs=[whole] * len(args),
        out_specs=jax.tree.map(lambda _: whole, out),
        scratch_shapes=scratch,
        compiler_params=pltpu.CompilerParams(vmem_limit_bytes=VMEM),
    )(*args)


def shape(*dims, dtype=BF):
    return jax.ShapeDtypeStruct(dims, dtype)


AHEAD = [(i, (i + 1) % 4) for i in range(4)]
BEHIND = [(i, (i + 3) % 4) for i in range(4)]


def ring(fwd, bwd):
    return lax.ppermute(fwd, "dp", AHEAD), lax.ppermute(bwd, "dp", BEHIND)


def second(parts, left, right):
    half = parts[2].shape[0]
    fwd = (parts[2].astype(F32) + left[:half].astype(F32)).astype(BF)
    bwd = (parts[3].astype(F32) + right[half:].astype(F32)).astype(BF)
    return fwd, bwd


def early(own, left, right):
    low = lax.broadcasted_iota(jnp.int32, own.shape, 0) < own.shape[0] // 2
    begun = own.astype(F32) + jnp.where(low, right, left).astype(F32)
    return lax.optimization_barrier(begun.astype(BF))


def total(begun, left2, right2):
    half, columns = left2.shape
    both = lambda a: jnp.broadcast_to(a[None], (2, half, columns))
    low = lax.broadcasted_iota(jnp.int32, (2, half, columns), 0) == 0
    then = jnp.where(low, both(left2), both(right2)).astype(F32)
    return (begun.reshape(2, half, columns).astype(F32) + then).astype(BF).reshape(2 * half, columns)


def after(value, earlier):
    return lax.optimization_barrier((value, earlier))[0]


def on_device(tokens_in, out_grad, gates, expert_ids, slot_ids, w_up, w_down):
    groups = lax.axis_size("chip")
    count, width = tokens_in.shape
    hidden = w_up.shape[2]
    rows = 9 * groups
    turn = pltpu.VMEM((groups, 8, LANES), F32)
    swap = [(0, 1), (1, 0)]
    sent = call(
        pack_kernel,
        shape(groups, 18, 8, LANES),
        [pltpu.VMEM((rows, width), F32), turn],
        tokens_in,
        out_grad,
        gates,
        expert_ids,
        slot_ids,
    )
    mine = lax.all_to_all(sent, "chip", split_axis=0, concat_axis=0, tiled=True)
    other = lax.ppermute(mine, "core", swap)

    def parts(length, columns):
        quarter = length // 4
        return (
            shape(quarter, columns),
            shape(quarter, columns),
            shape(quarter // 2, columns),
            shape(quarter // 2, columns),
            shape(quarter, columns),
        )

    with jax.named_scope("all"):
      keep, give, *both_parts = call(
        expert_kernel,
        (shape(groups, 10, 8, LANES), shape(groups, 10, 8, LANES)) + parts(hidden, width) + parts(width, hidden),
        [pltpu.VMEM((2 * rows, width), BF), pltpu.VMEM((2 * rows, hidden), BF), pltpu.VMEM((2 * rows, LANES), F32), pltpu.VMEM((2 * rows, width), BF),
            pltpu.VMEM((2 * rows, hidden), BF),
            pltpu.VMEM((2 * rows, hidden), F32),
            pltpu.VMEM((2 * rows, hidden), F32),
            turn,
        ],
        mine,
        other,
        w_up,
        w_down,
      )
    down, up = both_parts[:5], both_parts[5:]
    with jax.named_scope("down_one"):
      left_d, right_d = ring(down[0], down[1])
    with jax.named_scope("swap_back"):
      got = lax.ppermute(give, "core", swap)
    with jax.named_scope("up_one"):
      left_u, right_u = ring(up[0], up[1])
    both = (keep.astype(F32) + got.astype(F32)).astype(BF)
    with jax.named_scope("rows_back"):
      back = lax.all_to_all(both, "chip", split_axis=0, concat_axis=0, tiled=True)
    down2 = second(down, left_d, right_d)
    with jax.named_scope("down_two"):
      left_d2, right_d2 = ring(*down2)
    up2 = second(up, left_u, right_u)
    with jax.named_scope("up_two"):
      left_u2, right_u2 = ring(*up2)
    down_grad = total(early(down[4], left_d, right_d), left_d2, right_d2)
    with jax.named_scope("unpack"):
      in_grad, gate_grad = call(
          unpack_kernel,
          (shape(count, width), shape(count)),
          [pltpu.VMEM((rows, width), BF), turn],
          back,
          gates,
          expert_ids,
          slot_ids,
      )
    left_u2, right_u2, in_grad = lax.optimization_barrier((left_u2, right_u2, in_grad))
    left_u2, right_u2, down_grad = lax.optimization_barrier((left_u2, right_u2, down_grad))
    up_grad = total(early(up[4], left_u, right_u), left_u2, right_u2)
    return (in_grad, gate_grad, up_grad[None], down_grad[None])


def solution(mesh):
    chips = mesh.devices.reshape(mesh.shape["expert"] // 2, 2, mesh.shape["dp"])
    finer = Mesh(chips, ("chip", "core", "dp"))
    tokens = ("chip", "core", "dp")
    pieces = ("chip", "core")
    return jax.shard_map(
        on_device,
        mesh=finer,
        in_specs=(
            P(tokens, None),
            P(tokens, None),
            P(tokens),
            P(tokens),
            P(tokens),
            P(pieces, None, None),
            P(pieces, None, None),
        ),
        out_specs=(
            P(tokens, None),
            P(tokens),
            P(pieces, "dp", None),
            P(pieces, "dp", None),
        ),
        check_vma=False,
    )
```

```python
import functools

import jax
import jax.numpy as jnp
from jax import lax
from jax.experimental import pallas as pl
from jax.experimental.pallas import tpu as pltpu
from jax.sharding import Mesh, PartitionSpec as P

BF = jnp.bfloat16
F32 = jnp.float32
MIB = 1024 * 1024
LANES = 128


def matmul(a, b, contract):
    return lax.dot_general(a, b, (contract, ((), ())), preferred_element_type=F32)


def slot_row(expert, slot, groups):
    return jnp.where(slot < 8, expert * 8 + slot, 8 * groups + expert)


def to_tiles(get, out_ref, base, groups, turn):
    for j in range(8):
        part = get(0, 8 * groups, j)
        out_ref[:, base + j] = part.reshape(groups, 8, LANES).astype(BF)
        turn[:, j, :] = get(8 * groups, 9 * groups, j)
    out_ref[:, base + 8] = turn[...].astype(BF)


def from_tiles(ref, base, dst_ref, row, groups, turn):
    turn[...] = ref[:, base + 8].astype(F32)
    for j in range(8):
        cols = slice(LANES * j, LANES * (j + 1))
        part = ref[:, base + j].astype(F32).reshape(8 * groups, LANES)
        dst_ref[row : row + 8 * groups, cols] = part.astype(BF)
        dst_ref[row + 8 * groups : row + 9 * groups, cols] = turn[:, j, :].astype(BF)


def pack_kernel(x_ref, g_ref, gate_ref, expert_ref, slot_ref, out_ref, full, turn):
    groups = out_ref.shape[0]
    count = x_ref.shape[0]
    place = slot_row(expert_ref[...], slot_ref[...], groups).reshape(1, count)
    rows = lax.broadcasted_iota(jnp.int32, (9 * groups, count), 0)
    hit = rows == place
    gate = gate_ref[...].astype(F32).reshape(1, count)
    for side, (ref, scale) in enumerate(((x_ref, 1.0), (g_ref, gate))):
        pick = jnp.where(hit, scale, 0.0).astype(BF)
        full[...] = matmul(pick, ref[...], ((1,), (0,)))
        to_tiles(
            lambda a, b, j: full[a:b, LANES * j : LANES * (j + 1)],
            out_ref,
            9 * side,
            groups,
            turn,
        )


def weight_parts(lhs_ref, rhs, me, fwd1, bwd1, fwd2, bwd2, own):
    half = own.shape[0] // 2
    size = 2 * half

    def chunk(step):
        at = pl.multiple_of(lax.rem(me + step, 4) * size, size)
        return matmul(lhs_ref[:, pl.ds(at, size)], rhs, ((0,), (0,))).astype(BF)

    far = chunk(2)
    fwd1[:half] = far[:half]
    bwd1[half:] = far[half:]
    right = chunk(1)
    fwd1[half:] = right[half:]
    fwd2[...] = right[:half]
    left = chunk(3)
    bwd1[:half] = left[:half]
    bwd2[...] = left[half:]
    own[...] = chunk(0)


def unpacked(mine_ref, other_ref, xs, ds, turn):
    groups = mine_ref.shape[0]
    for part, ref in enumerate((mine_ref, other_ref)):
        from_tiles(ref, 0, xs, part * 9 * groups, groups, turn)
        from_tiles(ref, 9, ds, part * 9 * groups, groups, turn)


def activation(hid, dact, act, dh, gate):
    step = 64

    def block(i, carry):
        at = pl.ds(pl.multiple_of(i * step, step), step)
        total = None
        for start in range(0, hid.shape[1], LANES):
            cols = pl.ds(start, LANES)
            v = hid[at, cols]
            d = dact[at, cols]
            cdf = 0.5 * (1.0 + lax.erf(v * 0.7071067811865476))
            pdf = jnp.exp(-0.5 * v * v) * 0.3989422804014327
            a = (v * cdf).astype(BF)
            act[at, cols] = a
            dh[at, cols] = (d * (cdf + v * pdf)).astype(BF)
            part = a.astype(F32) * d
            total = part if total is None else total + part
        row = jnp.sum(total, axis=1, keepdims=True)
        gate[at, :] = jnp.broadcast_to(row, (step, LANES))
        return carry

    lax.fori_loop(0, hid.shape[0] // step, block, 0)


def returned(dh, gate, up_ref, mine_ref, other_ref, full, turn):
    groups = mine_ref.shape[0]
    rows = 9 * groups
    full[...] = matmul(dh[...], up_ref[0], ((1,), (1,)))
    lane = lax.broadcasted_iota(jnp.int32, (groups, 8, LANES), 2)
    for part, ref in enumerate((mine_ref, other_ref)):
        at = part * rows
        to_tiles(
            lambda a, b, j: full[at + a : at + b, LANES * j : LANES * (j + 1)], ref, 0, groups, turn
        )
        last = gate[at + 8 * groups : at + rows, :]
        for j in range(8):
            turn[:, j, :] = last
        first = gate[at : at + 8 * groups, :].reshape(groups, 8, LANES)
        ref[:, 9] = jnp.where(lane < 64, first, turn[...]).astype(BF)


def expert_kernel(
    mine_ref, other_ref, up_ref, down_ref, xs, dh, keep, give, fwd1, bwd1, fwd2, bwd2, own, gate, ds, act, hid, dact, turn
):
    unpacked(mine_ref, other_ref, xs, ds, turn)
    hid[...] = matmul(xs[...], up_ref[0], ((1,), (0,)))
    dact[...] = matmul(ds[...], down_ref[0], ((1,), (1,)))
    activation(hid, dact, act, dh, gate)
    weight_parts(act, ds[...], lax.axis_index("dp"), fwd1, bwd1, fwd2, bwd2, own)
    returned(dh, gate, up_ref, keep, give, hid, turn)


def up_kernel(xs, dh, fwd1, bwd1, fwd2, bwd2, own):
    weight_parts(xs, dh[...], lax.axis_index("dp"), fwd1, bwd1, fwd2, bwd2, own)


def unpack_kernel(back_ref, gate_ref, expert_ref, slot_ref, out_ref, gate_out_ref, rowbuf, turn):
    groups = back_ref.shape[0]
    count = out_ref.shape[0]
    from_tiles(back_ref, 0, rowbuf, 0, groups, turn)
    expert = expert_ref[...].reshape(1, count)
    slot = slot_ref[...].reshape(1, count)
    rows = lax.broadcasted_iota(jnp.int32, (9 * groups, count), 0)
    pick = jnp.where(rows == slot_row(expert, slot, groups), 1.0, 0.0).astype(BF)
    out_ref[...] = matmul(pick, rowbuf[...], ((0,), (0,))).astype(BF)
    gates = back_ref[:, 9].astype(F32).reshape(8 * groups, LANES).astype(BF)
    rows = lax.broadcasted_iota(jnp.int32, (8 * groups, count), 0)
    low = jnp.where(rows == slot_row(expert, slot, groups), 1.0, 0.0).astype(BF)
    high = jnp.where((rows == expert * 8) & (slot == 8), 1.0, 0.0).astype(BF)
    low = matmul(gates, low, ((0,), (0,)))
    high = matmul(gates, high, ((0,), (0,)))
    total = low[0:1, :] + high[64:65, :]
    gate = gate_ref[...].astype(F32).reshape(1, count)
    gate_out_ref[...] = (total / gate).astype(BF).reshape(count)


def call(kernel, room, out, scratch, *args):
    whole = pl.BlockSpec(memory_space=pltpu.VMEM)
    return pl.pallas_call(
        kernel,
        out_shape=out,
        in_specs=[whole] * len(args),
        out_specs=jax.tree.map(lambda _: whole, out),
        scratch_shapes=scratch,
        compiler_params=pltpu.CompilerParams(vmem_limit_bytes=room * MIB),
    )(*args)


def shape(*dims, dtype=BF):
    return jax.ShapeDtypeStruct(dims, dtype)


AHEAD = [(i, (i + 1) % 4) for i in range(4)]
BEHIND = [(i, (i + 3) % 4) for i in range(4)]


def ring(fwd, bwd):
    return lax.ppermute(fwd, "dp", AHEAD), lax.ppermute(bwd, "dp", BEHIND)


def second(parts, left, right):
    half = parts[2].shape[0]
    fwd = (parts[2].astype(F32) + left[:half].astype(F32)).astype(BF)
    bwd = (parts[3].astype(F32) + right[half:].astype(F32)).astype(BF)
    return fwd, bwd


def early(own, left, right):
    low = lax.broadcasted_iota(jnp.int32, own.shape, 0) < own.shape[0] // 2
    return lax.optimization_barrier(own.astype(F32) + jnp.where(low, right, left).astype(F32))


def total(begun, left2, right2):
    half, columns = left2.shape
    both = lambda a: jnp.broadcast_to(a[None], (2, half, columns))
    low = lax.broadcasted_iota(jnp.int32, (2, half, columns), 0) == 0
    then = jnp.where(low, both(left2), both(right2)).astype(F32)
    return (begun.reshape(2, half, columns) + then).astype(BF).reshape(2 * half, columns)


def after(value, earlier):
    return lax.optimization_barrier((value, earlier))[0]


def on_device(tokens_in, out_grad, gates, expert_ids, slot_ids, w_up, w_down):
    groups = lax.axis_size("chip")
    count, width = tokens_in.shape
    hidden = w_up.shape[2]
    rows = 9 * groups
    turn = pltpu.VMEM((groups, 8, LANES), F32)
    swap = [(0, 1), (1, 0)]
    sent = call(
        pack_kernel,
        10,
        shape(groups, 18, 8, LANES),
        [pltpu.VMEM((rows, width), F32), turn],
        tokens_in,
        out_grad,
        gates,
        expert_ids,
        slot_ids,
    )
    mine = lax.all_to_all(sent, "chip", split_axis=0, concat_axis=0, tiled=True)
    other = lax.ppermute(mine, "core", swap)

    def parts(length, columns):
        quarter = length // 4
        return (
            shape(quarter, columns),
            shape(quarter, columns),
            shape(quarter // 2, columns),
            shape(quarter // 2, columns),
            shape(quarter, columns),
        )

    with jax.named_scope("expert_input"):
      xs, dh, keep, give, *down = call(
        expert_kernel,
        28,
        (shape(2 * rows, width), shape(2 * rows, hidden), shape(groups, 10, 8, LANES), shape(groups, 10, 8, LANES))
        + parts(hidden, width),
        [pltpu.VMEM((2 * rows, LANES), F32), pltpu.VMEM((2 * rows, width), BF),
            pltpu.VMEM((2 * rows, hidden), BF),
            pltpu.VMEM((2 * rows, hidden), F32),
            pltpu.VMEM((2 * rows, hidden), F32),
            turn,
        ],
        mine,
        other,
        w_up,
        w_down,
      )
    with jax.named_scope("down_one"):
      left_d, right_d = ring(down[0], down[1])
    with jax.named_scope("swap_back"):
      got = lax.ppermute(give, "core", swap)
    with jax.named_scope("up"):
      up = call(up_kernel, 12, parts(width, hidden), [], xs, dh)
    with jax.named_scope("up_one"):
      left_u, right_u = ring(up[0], up[1])
    both = (keep.astype(F32) + got.astype(F32)).astype(BF)
    with jax.named_scope("rows_back"):
      back = lax.all_to_all(both, "chip", split_axis=0, concat_axis=0, tiled=True)
    down2 = second(down, left_d, right_d)
    with jax.named_scope("down_two"):
      left_d2, right_d2 = ring(*down2)
    up2 = second(up, left_u, right_u)
    with jax.named_scope("up_two"):
      left_u2, right_u2 = ring(*up2)
    down_grad = total(early(down[4], left_d, right_d), left_d2, right_d2)
    with jax.named_scope("unpack"):
      in_grad, gate_grad = call(
          unpack_kernel,
          8,
          (shape(count, width), shape(count)),
          [pltpu.VMEM((rows, width), BF), turn],
          back,
          gates,
          expert_ids,
          slot_ids,
      )
    left_u2, right_u2, in_grad = lax.optimization_barrier((left_u2, right_u2, in_grad))
    left_u2, right_u2, down_grad = lax.optimization_barrier((left_u2, right_u2, down_grad))
    up_grad = total(early(up[4], left_u, right_u), left_u2, right_u2)
    return (in_grad, gate_grad, up_grad[None], down_grad[None])


def solution(mesh):
    chips = mesh.devices.reshape(mesh.shape["expert"] // 2, 2, mesh.shape["dp"])
    finer = Mesh(chips, ("chip", "core", "dp"))
    tokens = ("chip", "core", "dp")
    pieces = ("chip", "core")
    return jax.shard_map(
        on_device,
        mesh=finer,
        in_specs=(
            P(tokens, None),
            P(tokens, None),
            P(tokens),
            P(tokens),
            P(tokens),
            P(pieces, None, None),
            P(pieces, None, None),
        ),
        out_specs=(
            P(tokens, None),
            P(tokens),
            P(pieces, "dp", None),
            P(pieces, "dp", None),
        ),
        check_vma=False,
    )
```

```python
import functools

import jax
import jax.numpy as jnp
from jax import lax
from jax.experimental import pallas as pl
from jax.experimental.pallas import tpu as pltpu
from jax.sharding import Mesh, PartitionSpec as P

BF = jnp.bfloat16
F32 = jnp.float32
MIB = 1024 * 1024
LANES = 128


def matmul(a, b, contract):
    return lax.dot_general(a, b, (contract, ((), ())), preferred_element_type=F32)


def slot_row(expert, slot, groups):
    return jnp.where(slot < 8, expert * 8 + slot, 8 * groups + expert)


def to_tiles(get, out_ref, base, groups, turn):
    for j in range(8):
        part = get(0, 8 * groups, j)
        out_ref[:, base + j] = part.reshape(groups, 8, LANES).astype(BF)
        turn[:, j, :] = get(8 * groups, 9 * groups, j)
    out_ref[:, base + 8] = turn[...].astype(BF)


def from_tiles(ref, base, dst_ref, row, groups, turn):
    turn[...] = ref[:, base + 8].astype(F32)
    for j in range(8):
        cols = slice(LANES * j, LANES * (j + 1))
        part = ref[:, base + j].astype(F32).reshape(8 * groups, LANES)
        dst_ref[row : row + 8 * groups, cols] = part.astype(BF)
        dst_ref[row + 8 * groups : row + 9 * groups, cols] = turn[:, j, :].astype(BF)


def pack_kernel(x_ref, g_ref, gate_ref, expert_ref, slot_ref, out_ref, full, turn):
    groups = out_ref.shape[0]
    count = x_ref.shape[0]
    place = slot_row(expert_ref[...], slot_ref[...], groups).reshape(1, count)
    rows = lax.broadcasted_iota(jnp.int32, (9 * groups, count), 0)
    hit = rows == place
    gate = gate_ref[...].astype(F32).reshape(1, count)
    for side, (ref, scale) in enumerate(((x_ref, 1.0), (g_ref, gate))):
        pick = jnp.where(hit, scale, 0.0).astype(BF)
        full[...] = matmul(pick, ref[...], ((1,), (0,)))
        to_tiles(
            lambda a, b, j: full[a:b, LANES * j : LANES * (j + 1)],
            out_ref,
            9 * side,
            groups,
            turn,
        )


def weight_parts(lhs_ref, rhs, me, fwd1, bwd1, fwd2, bwd2, own):
    half = own.shape[0] // 2
    size = 2 * half

    def chunk(step):
        at = pl.multiple_of(lax.rem(me + step, 4) * size, size)
        return matmul(lhs_ref[:, pl.ds(at, size)], rhs, ((0,), (0,))).astype(BF)

    far = chunk(2)
    fwd1[:half] = far[:half]
    bwd1[half:] = far[half:]
    right = chunk(1)
    fwd1[half:] = right[half:]
    fwd2[...] = right[:half]
    left = chunk(3)
    bwd1[:half] = left[:half]
    bwd2[...] = left[half:]
    own[...] = chunk(0)


def unpacked(mine_ref, other_ref, xs, ds, turn):
    groups = mine_ref.shape[0]
    for part, ref in enumerate((mine_ref, other_ref)):
        from_tiles(ref, 0, xs, part * 9 * groups, groups, turn)
        from_tiles(ref, 9, ds, part * 9 * groups, groups, turn)


def activation(hid, dact, act, dh, gate):
    step = 64

    def block(i, carry):
        at = pl.ds(pl.multiple_of(i * step, step), step)
        total = None
        for start in range(0, hid.shape[1], LANES):
            cols = pl.ds(start, LANES)
            v = hid[at, cols]
            d = dact[at, cols]
            cdf = 0.5 * (1.0 + lax.erf(v * 0.7071067811865476))
            pdf = jnp.exp(-0.5 * v * v) * 0.3989422804014327
            a = (v * cdf).astype(BF)
            act[at, cols] = a
            dh[at, cols] = (d * (cdf + v * pdf)).astype(BF)
            part = a.astype(F32) * d
            total = part if total is None else total + part
        row = jnp.sum(total, axis=1, keepdims=True)
        gate[at, :] = jnp.broadcast_to(row, (step, LANES))
        return carry

    lax.fori_loop(0, hid.shape[0] // step, block, 0)


def returned(dh, gate, up_ref, mine_ref, other_ref, full, turn):
    groups = mine_ref.shape[0]
    rows = 9 * groups
    full[...] = matmul(dh[...], up_ref[0], ((1,), (1,)))
    lane = lax.broadcasted_iota(jnp.int32, (groups, 8, LANES), 2)
    for part, ref in enumerate((mine_ref, other_ref)):
        at = part * rows
        to_tiles(
            lambda a, b, j: full[at + a : at + b, LANES * j : LANES * (j + 1)], ref, 0, groups, turn
        )
        last = gate[at + 8 * groups : at + rows, :]
        for j in range(8):
            turn[:, j, :] = last
        first = gate[at : at + 8 * groups, :].reshape(groups, 8, LANES)
        ref[:, 9] = jnp.where(lane < 64, first, turn[...]).astype(BF)


def expert_kernel(
    mine_ref, other_ref, up_ref, down_ref, xs, dh, keep, give, fwd1, bwd1, fwd2, bwd2, own, gate, ds, act, hid, dact, turn
):
    unpacked(mine_ref, other_ref, xs, ds, turn)
    hid[...] = matmul(xs[...], up_ref[0], ((1,), (0,)))
    dact[...] = matmul(ds[...], down_ref[0], ((1,), (1,)))
    activation(hid, dact, act, dh, gate)
    weight_parts(act, ds[...], lax.axis_index("dp"), fwd1, bwd1, fwd2, bwd2, own)
    returned(dh, gate, up_ref, keep, give, hid, turn)


def up_kernel(xs, dh, fwd1, bwd1, fwd2, bwd2, own):
    weight_parts(xs, dh[...], lax.axis_index("dp"), fwd1, bwd1, fwd2, bwd2, own)


def unpack_kernel(back_ref, gate_ref, expert_ref, slot_ref, out_ref, gate_out_ref, rowbuf, turn):
    groups = back_ref.shape[0]
    count = out_ref.shape[0]
    from_tiles(back_ref, 0, rowbuf, 0, groups, turn)
    expert = expert_ref[...].reshape(1, count)
    slot = slot_ref[...].reshape(1, count)
    rows = lax.broadcasted_iota(jnp.int32, (9 * groups, count), 0)
    pick = jnp.where(rows == slot_row(expert, slot, groups), 1.0, 0.0).astype(BF)
    out_ref[...] = matmul(pick, rowbuf[...], ((0,), (0,))).astype(BF)
    gates = back_ref[:, 9].astype(F32).reshape(8 * groups, LANES).astype(BF)
    rows = lax.broadcasted_iota(jnp.int32, (8 * groups, count), 0)
    low = jnp.where(rows == slot_row(expert, slot, groups), 1.0, 0.0).astype(BF)
    high = jnp.where((rows == expert * 8) & (slot == 8), 1.0, 0.0).astype(BF)
    low = matmul(gates, low, ((0,), (0,)))
    high = matmul(gates, high, ((0,), (0,)))
    total = low[0:1, :] + high[64:65, :]
    gate = gate_ref[...].astype(F32).reshape(1, count)
    gate_out_ref[...] = (total / gate).astype(BF).reshape(count)


def call(kernel, room, out, scratch, *args):
    whole = pl.BlockSpec(memory_space=pltpu.VMEM)
    return pl.pallas_call(
        kernel,
        out_shape=out,
        in_specs=[whole] * len(args),
        out_specs=jax.tree.map(lambda _: whole, out),
        scratch_shapes=scratch,
        compiler_params=pltpu.CompilerParams(vmem_limit_bytes=room * MIB),
    )(*args)


def shape(*dims, dtype=BF):
    return jax.ShapeDtypeStruct(dims, dtype)


AHEAD = [(i, (i + 1) % 4) for i in range(4)]
BEHIND = [(i, (i + 3) % 4) for i in range(4)]


def ring(fwd, bwd):
    return lax.ppermute(fwd, "dp", AHEAD), lax.ppermute(bwd, "dp", BEHIND)


def second(parts, left, right):
    half = parts[2].shape[0]
    fwd = (parts[2].astype(F32) + left[:half].astype(F32)).astype(BF)
    bwd = (parts[3].astype(F32) + right[half:].astype(F32)).astype(BF)
    return fwd, bwd


def total(own, left, right, left2, right2):
    half, columns = left2.shape
    split = lambda a: a.reshape(2, half, columns)
    both = lambda a: jnp.broadcast_to(a[None], (2, half, columns))
    low = lax.broadcasted_iota(jnp.int32, (2, half, columns), 0) == 0
    first = jnp.where(low, split(right), split(left)).astype(F32)
    then = jnp.where(low, both(left2), both(right2)).astype(F32)
    return (split(own).astype(F32) + first + then).astype(BF).reshape(2 * half, columns)


def after(value, earlier):
    return lax.optimization_barrier((value, earlier))[0]


def on_device(tokens_in, out_grad, gates, expert_ids, slot_ids, w_up, w_down):
    groups = lax.axis_size("chip")
    count, width = tokens_in.shape
    hidden = w_up.shape[2]
    rows = 9 * groups
    turn = pltpu.VMEM((groups, 8, LANES), F32)
    swap = [(0, 1), (1, 0)]
    sent = call(
        pack_kernel,
        56,
        shape(groups, 18, 8, LANES),
        [pltpu.VMEM((rows, width), F32), turn],
        tokens_in,
        out_grad,
        gates,
        expert_ids,
        slot_ids,
    )
    mine = lax.all_to_all(sent, "chip", split_axis=0, concat_axis=0, tiled=True)
    other = lax.ppermute(mine, "core", swap)

    def parts(length, columns):
        quarter = length // 4
        return (
            shape(quarter, columns),
            shape(quarter, columns),
            shape(quarter // 2, columns),
            shape(quarter // 2, columns),
            shape(quarter, columns),
        )

    with jax.named_scope("expert_input"):
      xs, dh, keep, give, *down = call(
        expert_kernel,
        28,
        (shape(2 * rows, width), shape(2 * rows, hidden), shape(groups, 10, 8, LANES), shape(groups, 10, 8, LANES))
        + parts(hidden, width),
        [pltpu.VMEM((2 * rows, LANES), F32), pltpu.VMEM((2 * rows, width), BF),
            pltpu.VMEM((2 * rows, hidden), BF),
            pltpu.VMEM((2 * rows, hidden), F32),
            pltpu.VMEM((2 * rows, hidden), F32),
            turn,
        ],
        mine,
        other,
        w_up,
        w_down,
      )
    with jax.named_scope("down_one"):
      left_d, right_d = ring(down[0], down[1])
    with jax.named_scope("swap_back"):
      got = lax.ppermute(give, "core", swap)
    with jax.named_scope("up"):
      up = call(up_kernel, 12, parts(width, hidden), [], xs, dh)
    with jax.named_scope("up_one"):
      left_u, right_u = ring(up[0], up[1])
    both = (keep.astype(F32) + got.astype(F32)).astype(BF)
    with jax.named_scope("rows_back"):
      back = lax.all_to_all(both, "chip", split_axis=0, concat_axis=0, tiled=True)
    down2 = second(down, left_d, right_d)
    with jax.named_scope("down_two"):
      left_d2, right_d2 = ring(*down2)
    up2 = second(up, left_u, right_u)
    with jax.named_scope("up_two"):
      left_u2, right_u2 = ring(*up2)
    down_grad = total(down[4], left_d, right_d, left_d2, right_d2)
    with jax.named_scope("unpack"):
      in_grad, gate_grad = call(
          unpack_kernel,
          8,
          (shape(count, width), shape(count)),
          [pltpu.VMEM((rows, width), BF), turn],
          back,
          gates,
          expert_ids,
          slot_ids,
      )
    left_u2, right_u2, in_grad = lax.optimization_barrier((left_u2, right_u2, in_grad))
    left_u2, right_u2, down_grad = lax.optimization_barrier((left_u2, right_u2, down_grad))
    up_grad = total(up[4], left_u, right_u, left_u2, right_u2)
    return (in_grad, gate_grad, up_grad[None], down_grad[None])


def solution(mesh):
    chips = mesh.devices.reshape(mesh.shape["expert"] // 2, 2, mesh.shape["dp"])
    finer = Mesh(chips, ("chip", "core", "dp"))
    tokens = ("chip", "core", "dp")
    pieces = ("chip", "core")
    return jax.shard_map(
        on_device,
        mesh=finer,
        in_specs=(
            P(tokens, None),
            P(tokens, None),
            P(tokens),
            P(tokens),
            P(tokens),
            P(pieces, None, None),
            P(pieces, None, None),
        ),
        out_specs=(
            P(tokens, None),
            P(tokens),
            P(pieces, "dp", None),
            P(pieces, "dp", None),
        ),
        check_vma=False,
    )
```

```python
import functools

import jax
import jax.numpy as jnp
from jax import lax
from jax.experimental import pallas as pl
from jax.experimental.pallas import tpu as pltpu
from jax.sharding import Mesh, PartitionSpec as P

BF = jnp.bfloat16
F32 = jnp.float32
MIB = 1024 * 1024
LANES = 128


def matmul(a, b, contract):
    return lax.dot_general(a, b, (contract, ((), ())), preferred_element_type=F32)


def slot_row(expert, slot, groups):
    return jnp.where(slot < 8, expert * 8 + slot, 8 * groups + expert)


def to_tiles(get, out_ref, base, groups, turn):
    for j in range(8):
        part = get(0, 8 * groups, j)
        out_ref[:, base + j] = part.reshape(groups, 8, LANES).astype(BF)
        turn[:, j, :] = get(8 * groups, 9 * groups, j)
    out_ref[:, base + 8] = turn[...].astype(BF)


def from_tiles(ref, base, dst_ref, row, groups, turn):
    turn[...] = ref[:, base + 8].astype(F32)
    for j in range(8):
        cols = slice(LANES * j, LANES * (j + 1))
        part = ref[:, base + j].astype(F32).reshape(8 * groups, LANES)
        dst_ref[row : row + 8 * groups, cols] = part.astype(BF)
        dst_ref[row + 8 * groups : row + 9 * groups, cols] = turn[:, j, :].astype(BF)


def pack_kernel(x_ref, g_ref, gate_ref, expert_ref, slot_ref, out_ref, full, turn):
    groups = out_ref.shape[0]
    count = x_ref.shape[0]
    place = slot_row(expert_ref[...], slot_ref[...], groups).reshape(1, count)
    rows = lax.broadcasted_iota(jnp.int32, (9 * groups, count), 0)
    hit = rows == place
    gate = gate_ref[...].astype(F32).reshape(1, count)
    for side, (ref, scale) in enumerate(((x_ref, 1.0), (g_ref, gate))):
        pick = jnp.where(hit, scale, 0.0).astype(BF)
        full[...] = matmul(pick, ref[...], ((1,), (0,)))
        to_tiles(
            lambda a, b, j: full[a:b, LANES * j : LANES * (j + 1)],
            out_ref,
            9 * side,
            groups,
            turn,
        )


def weight_parts(lhs_ref, rhs, me, fwd1, bwd1, fwd2, bwd2, own):
    half = own.shape[0] // 2
    size = 2 * half

    def chunk(step):
        at = pl.multiple_of(lax.rem(me + step, 4) * size, size)
        return matmul(lhs_ref[:, pl.ds(at, size)], rhs, ((0,), (0,))).astype(BF)

    far = chunk(2)
    fwd1[:half] = far[:half]
    bwd1[half:] = far[half:]
    right = chunk(1)
    fwd1[half:] = right[half:]
    fwd2[...] = right[:half]
    left = chunk(3)
    bwd1[:half] = left[:half]
    bwd2[...] = left[half:]
    own[...] = chunk(0)


def unpacked(mine_ref, other_ref, xs, ds, turn):
    groups = mine_ref.shape[0]
    for part, ref in enumerate((mine_ref, other_ref)):
        from_tiles(ref, 0, xs, part * 9 * groups, groups, turn)
        from_tiles(ref, 9, ds, part * 9 * groups, groups, turn)


def activation(hid, dact, act, dh, gate):
    step = 64

    def block(i, carry):
        at = pl.ds(pl.multiple_of(i * step, step), step)
        total = None
        for start in range(0, hid.shape[1], LANES):
            cols = pl.ds(start, LANES)
            v = hid[at, cols]
            d = dact[at, cols]
            cdf = 0.5 * (1.0 + lax.erf(v * 0.7071067811865476))
            pdf = jnp.exp(-0.5 * v * v) * 0.3989422804014327
            a = (v * cdf).astype(BF)
            act[at, cols] = a
            dh[at, cols] = (d * (cdf + v * pdf)).astype(BF)
            part = a.astype(F32) * d
            total = part if total is None else total + part
        row = jnp.sum(total, axis=1, keepdims=True)
        gate[at, :] = jnp.broadcast_to(row, (step, LANES))
        return carry

    lax.fori_loop(0, hid.shape[0] // step, block, 0)


def returned(dh, gate, up_ref, mine_ref, other_ref, full, turn):
    groups = mine_ref.shape[0]
    rows = 9 * groups
    full[...] = matmul(dh[...], up_ref[0], ((1,), (1,)))
    lane = lax.broadcasted_iota(jnp.int32, (groups, 8, LANES), 2)
    for part, ref in enumerate((mine_ref, other_ref)):
        at = part * rows
        to_tiles(
            lambda a, b, j: full[at + a : at + b, LANES * j : LANES * (j + 1)], ref, 0, groups, turn
        )
        last = gate[at + 8 * groups : at + rows, :]
        for j in range(8):
            turn[:, j, :] = last
        first = gate[at : at + 8 * groups, :].reshape(groups, 8, LANES)
        ref[:, 9] = jnp.where(lane < 64, first, turn[...]).astype(BF)


def expert_kernel(
    mine_ref, other_ref, up_ref, down_ref, xs, dh, keep, give, fwd1, bwd1, fwd2, bwd2, own, gate, ds, act, hid, dact, turn
):
    unpacked(mine_ref, other_ref, xs, ds, turn)
    hid[...] = matmul(xs[...], up_ref[0], ((1,), (0,)))
    dact[...] = matmul(ds[...], down_ref[0], ((1,), (1,)))
    activation(hid, dact, act, dh, gate)
    weight_parts(act, ds[...], lax.axis_index("dp"), fwd1, bwd1, fwd2, bwd2, own)
    returned(dh, gate, up_ref, keep, give, hid, turn)


def up_kernel(xs, dh, fwd1, bwd1, fwd2, bwd2, own):
    weight_parts(xs, dh[...], lax.axis_index("dp"), fwd1, bwd1, fwd2, bwd2, own)


def unpack_kernel(back_ref, gate_ref, expert_ref, slot_ref, out_ref, gate_out_ref, rowbuf, turn):
    groups = back_ref.shape[0]
    count = out_ref.shape[0]
    from_tiles(back_ref, 0, rowbuf, 0, groups, turn)
    expert = expert_ref[...].reshape(1, count)
    slot = slot_ref[...].reshape(1, count)
    rows = lax.broadcasted_iota(jnp.int32, (9 * groups, count), 0)
    pick = jnp.where(rows == slot_row(expert, slot, groups), 1.0, 0.0).astype(BF)
    out_ref[...] = matmul(pick, rowbuf[...], ((0,), (0,))).astype(BF)
    gates = back_ref[:, 9].astype(F32).reshape(8 * groups, LANES).astype(BF)
    rows = lax.broadcasted_iota(jnp.int32, (8 * groups, count), 0)
    low = jnp.where(rows == slot_row(expert, slot, groups), 1.0, 0.0).astype(BF)
    high = jnp.where((rows == expert * 8) & (slot == 8), 1.0, 0.0).astype(BF)
    low = matmul(gates, low, ((0,), (0,)))
    high = matmul(gates, high, ((0,), (0,)))
    total = low[0:1, :] + high[64:65, :]
    gate = gate_ref[...].astype(F32).reshape(1, count)
    gate_out_ref[...] = (total / gate).astype(BF).reshape(count)


def call(kernel, room, out, scratch, *args):
    whole = pl.BlockSpec(memory_space=pltpu.VMEM)
    return pl.pallas_call(
        kernel,
        out_shape=out,
        in_specs=[whole] * len(args),
        out_specs=jax.tree.map(lambda _: whole, out),
        scratch_shapes=scratch,
        compiler_params=pltpu.CompilerParams(vmem_limit_bytes=room * MIB),
    )(*args)


def shape(*dims, dtype=BF):
    return jax.ShapeDtypeStruct(dims, dtype)


AHEAD = [(i, (i + 1) % 4) for i in range(4)]
BEHIND = [(i, (i + 3) % 4) for i in range(4)]


def ring(fwd, bwd):
    return lax.ppermute(fwd, "dp", AHEAD), lax.ppermute(bwd, "dp", BEHIND)


def second(parts, left, right):
    half = parts[2].shape[0]
    fwd = (parts[2].astype(F32) + left[:half].astype(F32)).astype(BF)
    bwd = (parts[3].astype(F32) + right[half:].astype(F32)).astype(BF)
    return fwd, bwd


def early(own, left, right):
    low = lax.broadcasted_iota(jnp.int32, own.shape, 0) < own.shape[0] // 2
    begun = own.astype(F32) + jnp.where(low, right, left).astype(F32)
    return lax.optimization_barrier(begun.astype(BF))


def total(begun, left2, right2):
    half, columns = left2.shape
    both = lambda a: jnp.broadcast_to(a[None], (2, half, columns))
    low = lax.broadcasted_iota(jnp.int32, (2, half, columns), 0) == 0
    then = jnp.where(low, both(left2), both(right2)).astype(F32)
    return (begun.reshape(2, half, columns).astype(F32) + then).astype(BF).reshape(2 * half, columns)


def after(value, earlier):
    return lax.optimization_barrier((value, earlier))[0]


def on_device(tokens_in, out_grad, gates, expert_ids, slot_ids, w_up, w_down):
    groups = lax.axis_size("chip")
    count, width = tokens_in.shape
    hidden = w_up.shape[2]
    rows = 9 * groups
    turn = pltpu.VMEM((groups, 8, LANES), F32)
    swap = [(0, 1), (1, 0)]
    sent = call(
        pack_kernel,
        56,
        shape(groups, 18, 8, LANES),
        [pltpu.VMEM((rows, width), F32), turn],
        tokens_in,
        out_grad,
        gates,
        expert_ids,
        slot_ids,
    )
    mine = lax.all_to_all(sent, "chip", split_axis=0, concat_axis=0, tiled=True)
    other = lax.ppermute(mine, "core", swap)

    def parts(length, columns):
        quarter = length // 4
        return (
            shape(quarter, columns),
            shape(quarter, columns),
            shape(quarter // 2, columns),
            shape(quarter // 2, columns),
            shape(quarter, columns),
        )

    with jax.named_scope("expert_input"):
      xs, dh, keep, give, *down = call(
        expert_kernel,
        28,
        (shape(2 * rows, width), shape(2 * rows, hidden), shape(groups, 10, 8, LANES), shape(groups, 10, 8, LANES))
        + parts(hidden, width),
        [pltpu.VMEM((2 * rows, LANES), F32), pltpu.VMEM((2 * rows, width), BF),
            pltpu.VMEM((2 * rows, hidden), BF),
            pltpu.VMEM((2 * rows, hidden), F32),
            pltpu.VMEM((2 * rows, hidden), F32),
            turn,
        ],
        mine,
        other,
        w_up,
        w_down,
      )
    with jax.named_scope("down_one"):
      left_d, right_d = ring(down[0], down[1])
    with jax.named_scope("swap_back"):
      got = lax.ppermute(give, "core", swap)
    with jax.named_scope("up"):
      up = call(up_kernel, 12, parts(width, hidden), [], xs, dh)
    with jax.named_scope("up_one"):
      left_u, right_u = ring(up[0], up[1])
    both = (keep.astype(F32) + got.astype(F32)).astype(BF)
    with jax.named_scope("rows_back"):
      back = lax.all_to_all(both, "chip", split_axis=0, concat_axis=0, tiled=True)
    down2 = second(down, left_d, right_d)
    with jax.named_scope("down_two"):
      left_d2, right_d2 = ring(*down2)
    up2 = second(up, left_u, right_u)
    with jax.named_scope("up_two"):
      left_u2, right_u2 = ring(*up2)
    down_grad = total(early(down[4], left_d, right_d), left_d2, right_d2)
    with jax.named_scope("unpack"):
      in_grad, gate_grad = call(
          unpack_kernel,
          8,
          (shape(count, width), shape(count)),
          [pltpu.VMEM((rows, width), BF), turn],
          back,
          gates,
          expert_ids,
          slot_ids,
      )
    left_u2, right_u2, in_grad = lax.optimization_barrier((left_u2, right_u2, in_grad))
    left_u2, right_u2, down_grad = lax.optimization_barrier((left_u2, right_u2, down_grad))
    up_grad = total(early(up[4], left_u, right_u), left_u2, right_u2)
    return (in_grad, gate_grad, up_grad[None], down_grad[None])


def solution(mesh):
    chips = mesh.devices.reshape(mesh.shape["expert"] // 2, 2, mesh.shape["dp"])
    finer = Mesh(chips, ("chip", "core", "dp"))
    tokens = ("chip", "core", "dp")
    pieces = ("chip", "core")
    return jax.shard_map(
        on_device,
        mesh=finer,
        in_specs=(
            P(tokens, None),
            P(tokens, None),
            P(tokens),
            P(tokens),
            P(tokens),
            P(pieces, None, None),
            P(pieces, None, None),
        ),
        out_specs=(
            P(tokens, None),
            P(tokens),
            P(pieces, "dp", None),
            P(pieces, "dp", None),
        ),
        check_vma=False,
    )
```

```python
import functools

import jax
import jax.numpy as jnp
from jax import lax
from jax.experimental import pallas as pl
from jax.experimental.pallas import tpu as pltpu
from jax.sharding import Mesh, PartitionSpec as P

BF = jnp.bfloat16
F32 = jnp.float32
MIB = 1024 * 1024
LANES = 128


def matmul(a, b, contract):
    return lax.dot_general(a, b, (contract, ((), ())), preferred_element_type=F32)


def slot_row(expert, slot, groups):
    return jnp.where(slot < 8, expert * 8 + slot, 8 * groups + expert)


def to_tiles(get, out_ref, base, groups, turn):
    for j in range(8):
        part = get(0, 8 * groups, j)
        out_ref[:, base + j] = part.reshape(groups, 8, LANES).astype(BF)
        turn[:, j, :] = get(8 * groups, 9 * groups, j)
    out_ref[:, base + 8] = turn[...].astype(BF)


def from_tiles(ref, base, dst_ref, row, groups, turn):
    turn[...] = ref[:, base + 8].astype(F32)
    for j in range(8):
        cols = slice(LANES * j, LANES * (j + 1))
        part = ref[:, base + j].astype(F32).reshape(8 * groups, LANES)
        dst_ref[row : row + 8 * groups, cols] = part.astype(BF)
        dst_ref[row + 8 * groups : row + 9 * groups, cols] = turn[:, j, :].astype(BF)


def pack_kernel(x_ref, g_ref, gate_ref, expert_ref, slot_ref, out_ref, full, turn):
    groups = out_ref.shape[0]
    count = x_ref.shape[0]
    place = slot_row(expert_ref[...], slot_ref[...], groups).reshape(1, count)
    rows = lax.broadcasted_iota(jnp.int32, (9 * groups, count), 0)
    hit = rows == place
    gate = gate_ref[...].astype(F32).reshape(1, count)
    for side, (ref, scale) in enumerate(((x_ref, 1.0), (g_ref, gate))):
        pick = jnp.where(hit, scale, 0.0).astype(BF)
        full[...] = matmul(pick, ref[...], ((1,), (0,)))
        to_tiles(
            lambda a, b, j: full[a:b, LANES * j : LANES * (j + 1)],
            out_ref,
            9 * side,
            groups,
            turn,
        )


def weight_parts(lhs_ref, rhs, me, fwd1, bwd1, fwd2, bwd2, own):
    half = own.shape[0] // 2
    size = 2 * half

    def chunk(step):
        at = pl.multiple_of(lax.rem(me + step, 4) * size, size)
        return matmul(lhs_ref[:, pl.ds(at, size)], rhs, ((0,), (0,))).astype(BF)

    far = chunk(2)
    fwd1[:half] = far[:half]
    bwd1[half:] = far[half:]
    right = chunk(1)
    fwd1[half:] = right[half:]
    fwd2[...] = right[:half]
    left = chunk(3)
    bwd1[:half] = left[:half]
    bwd2[...] = left[half:]
    own[...] = chunk(0)


def unpacked(mine_ref, other_ref, xs, ds, turn):
    groups = mine_ref.shape[0]
    for part, ref in enumerate((mine_ref, other_ref)):
        from_tiles(ref, 0, xs, part * 9 * groups, groups, turn)
        from_tiles(ref, 9, ds, part * 9 * groups, groups, turn)


def activation(hid, dact, act, dh, gate):
    step = 64

    def block(i, carry):
        at = pl.ds(pl.multiple_of(i * step, step), step)
        total = None
        for start in range(0, hid.shape[1], LANES):
            cols = pl.ds(start, LANES)
            v = hid[at, cols]
            d = dact[at, cols]
            cdf = 0.5 * (1.0 + lax.erf(v * 0.7071067811865476))
            pdf = jnp.exp(-0.5 * v * v) * 0.3989422804014327
            a = (v * cdf).astype(BF)
            act[at, cols] = a
            dh[at, cols] = (d * (cdf + v * pdf)).astype(BF)
            part = a.astype(F32) * d
            total = part if total is None else total + part
        row = jnp.sum(total, axis=1, keepdims=True)
        gate[at, :] = jnp.broadcast_to(row, (step, LANES))
        return carry

    lax.fori_loop(0, hid.shape[0] // step, block, 0)


def returned(dh, gate, up_ref, mine_ref, other_ref, full, turn):
    groups = mine_ref.shape[0]
    rows = 9 * groups
    full[...] = matmul(dh[...], up_ref[0], ((1,), (1,)))
    lane = lax.broadcasted_iota(jnp.int32, (groups, 8, LANES), 2)
    for part, ref in enumerate((mine_ref, other_ref)):
        at = part * rows
        to_tiles(
            lambda a, b, j: full[at + a : at + b, LANES * j : LANES * (j + 1)], ref, 0, groups, turn
        )
        last = gate[at + 8 * groups : at + rows, :]
        for j in range(8):
            turn[:, j, :] = last
        first = gate[at : at + 8 * groups, :].reshape(groups, 8, LANES)
        ref[:, 9] = jnp.where(lane < 64, first, turn[...]).astype(BF)


def expert_kernel(
    mine_ref, other_ref, up_ref, down_ref, keep, give, fwd1, bwd1, fwd2, bwd2, own, ufwd1, ubwd1, ufwd2, ubwd2, uown, xs, dh, gate, ds, act, hid, dact, turn
):
    unpacked(mine_ref, other_ref, xs, ds, turn)
    hid[...] = matmul(xs[...], up_ref[0], ((1,), (0,)))
    dact[...] = matmul(ds[...], down_ref[0], ((1,), (1,)))
    activation(hid, dact, act, dh, gate)
    weight_parts(act, ds[...], lax.axis_index("dp"), fwd1, bwd1, fwd2, bwd2, own)
    weight_parts(xs, dh[...], lax.axis_index("dp"), ufwd1, ubwd1, ufwd2, ubwd2, uown)
    returned(dh, gate, up_ref, keep, give, hid, turn)


def unpack_kernel(back_ref, gate_ref, expert_ref, slot_ref, out_ref, gate_out_ref, rowbuf, turn):
    groups = back_ref.shape[0]
    count = out_ref.shape[0]
    from_tiles(back_ref, 0, rowbuf, 0, groups, turn)
    expert = expert_ref[...].reshape(1, count)
    slot = slot_ref[...].reshape(1, count)
    rows = lax.broadcasted_iota(jnp.int32, (9 * groups, count), 0)
    pick = jnp.where(rows == slot_row(expert, slot, groups), 1.0, 0.0).astype(BF)
    out_ref[...] = matmul(pick, rowbuf[...], ((0,), (0,))).astype(BF)
    gates = back_ref[:, 9].astype(F32).reshape(8 * groups, LANES).astype(BF)
    rows = lax.broadcasted_iota(jnp.int32, (8 * groups, count), 0)
    low = jnp.where(rows == slot_row(expert, slot, groups), 1.0, 0.0).astype(BF)
    high = jnp.where((rows == expert * 8) & (slot == 8), 1.0, 0.0).astype(BF)
    low = matmul(gates, low, ((0,), (0,)))
    high = matmul(gates, high, ((0,), (0,)))
    total = low[0:1, :] + high[64:65, :]
    gate = gate_ref[...].astype(F32).reshape(1, count)
    gate_out_ref[...] = (total / gate).astype(BF).reshape(count)


def call(kernel, room, out, scratch, *args):
    whole = pl.BlockSpec(memory_space=pltpu.VMEM)
    return pl.pallas_call(
        kernel,
        out_shape=out,
        in_specs=[whole] * len(args),
        out_specs=jax.tree.map(lambda _: whole, out),
        scratch_shapes=scratch,
        compiler_params=pltpu.CompilerParams(vmem_limit_bytes=room * MIB),
    )(*args)


def shape(*dims, dtype=BF):
    return jax.ShapeDtypeStruct(dims, dtype)


AHEAD = [(i, (i + 1) % 4) for i in range(4)]
BEHIND = [(i, (i + 3) % 4) for i in range(4)]


def ring(fwd, bwd):
    return lax.ppermute(fwd, "dp", AHEAD), lax.ppermute(bwd, "dp", BEHIND)


def second(parts, left, right):
    half = parts[2].shape[0]
    fwd = (parts[2].astype(F32) + left[:half].astype(F32)).astype(BF)
    bwd = (parts[3].astype(F32) + right[half:].astype(F32)).astype(BF)
    return fwd, bwd


def early(own, left, right):
    low = lax.broadcasted_iota(jnp.int32, own.shape, 0) < own.shape[0] // 2
    begun = own.astype(F32) + jnp.where(low, right, left).astype(F32)
    return lax.optimization_barrier(begun.astype(BF))


def total(begun, left2, right2):
    half, columns = left2.shape
    both = lambda a: jnp.broadcast_to(a[None], (2, half, columns))
    low = lax.broadcasted_iota(jnp.int32, (2, half, columns), 0) == 0
    then = jnp.where(low, both(left2), both(right2)).astype(F32)
    return (begun.reshape(2, half, columns).astype(F32) + then).astype(BF).reshape(2 * half, columns)


def after(value, earlier):
    return lax.optimization_barrier((value, earlier))[0]


def on_device(tokens_in, out_grad, gates, expert_ids, slot_ids, w_up, w_down):
    groups = lax.axis_size("chip")
    count, width = tokens_in.shape
    hidden = w_up.shape[2]
    rows = 9 * groups
    turn = pltpu.VMEM((groups, 8, LANES), F32)
    swap = [(0, 1), (1, 0)]
    sent = call(
        pack_kernel,
        56,
        shape(groups, 18, 8, LANES),
        [pltpu.VMEM((rows, width), F32), turn],
        tokens_in,
        out_grad,
        gates,
        expert_ids,
        slot_ids,
    )
    mine = lax.all_to_all(sent, "chip", split_axis=0, concat_axis=0, tiled=True)
    other = lax.ppermute(mine, "core", swap)

    def parts(length, columns):
        quarter = length // 4
        return (
            shape(quarter, columns),
            shape(quarter, columns),
            shape(quarter // 2, columns),
            shape(quarter // 2, columns),
            shape(quarter, columns),
        )

    with jax.named_scope("all"):
      keep, give, *both_parts = call(
        expert_kernel,
        28,
        (shape(groups, 10, 8, LANES), shape(groups, 10, 8, LANES)) + parts(hidden, width) + parts(width, hidden),
        [pltpu.VMEM((2 * rows, width), BF), pltpu.VMEM((2 * rows, hidden), BF), pltpu.VMEM((2 * rows, LANES), F32), pltpu.VMEM((2 * rows, width), BF),
            pltpu.VMEM((2 * rows, hidden), BF),
            pltpu.VMEM((2 * rows, hidden), F32),
            pltpu.VMEM((2 * rows, hidden), F32),
            turn,
        ],
        mine,
        other,
        w_up,
        w_down,
      )
    down, up = both_parts[:5], both_parts[5:]
    with jax.named_scope("down_one"):
      left_d, right_d = ring(down[0], down[1])
    with jax.named_scope("swap_back"):
      got = lax.ppermute(give, "core", swap)
    with jax.named_scope("up_one"):
      left_u, right_u = ring(up[0], up[1])
    both = (keep.astype(F32) + got.astype(F32)).astype(BF)
    with jax.named_scope("rows_back"):
      back = lax.all_to_all(both, "chip", split_axis=0, concat_axis=0, tiled=True)
    down2 = second(down, left_d, right_d)
    with jax.named_scope("down_two"):
      left_d2, right_d2 = ring(*down2)
    up2 = second(up, left_u, right_u)
    with jax.named_scope("up_two"):
      left_u2, right_u2 = ring(*up2)
    down_grad = total(early(down[4], left_d, right_d), left_d2, right_d2)
    with jax.named_scope("unpack"):
      in_grad, gate_grad = call(
          unpack_kernel,
          8,
          (shape(count, width), shape(count)),
          [pltpu.VMEM((rows, width), BF), turn],
          back,
          gates,
          expert_ids,
          slot_ids,
      )
    left_u2, right_u2, in_grad = lax.optimization_barrier((left_u2, right_u2, in_grad))
    left_u2, right_u2, down_grad = lax.optimization_barrier((left_u2, right_u2, down_grad))
    up_grad = total(early(up[4], left_u, right_u), left_u2, right_u2)
    return (in_grad, gate_grad, up_grad[None], down_grad[None])


def solution(mesh):
    chips = mesh.devices.reshape(mesh.shape["expert"] // 2, 2, mesh.shape["dp"])
    finer = Mesh(chips, ("chip", "core", "dp"))
    tokens = ("chip", "core", "dp")
    pieces = ("chip", "core")
    return jax.shard_map(
        on_device,
        mesh=finer,
        in_specs=(
            P(tokens, None),
            P(tokens, None),
            P(tokens),
            P(tokens),
            P(tokens),
            P(pieces, None, None),
            P(pieces, None, None),
        ),
        out_specs=(
            P(tokens, None),
            P(tokens),
            P(pieces, "dp", None),
            P(pieces, "dp", None),
        ),
        check_vma=False,
    )
```
